256 devices in a mesh: sec: 4 (over z_hi, core), gx: 16 (over z_lo, y), gy: 4 (over x).
Axes of the slice: x: 4, y: 4, z: 8 (z_hi: 2, z_lo: 4; z = z_hi * 4 + z_lo), core: 2. Of those that a mesh axis runs over, the one named last changes fastest.
Arguments:
- fields: float32 [4, 3, 256, 8192], P('sec', None, 'gx', 'gy'), may hold values from -6 to 6
- x_ops: float32 [4, 3, 256, 256], P(None, None, 'gx'), may hold values from -4 to 4, as said below
- y_ops: float32 [4, 3, 256, 256], P(None, None, 'gy'), may hold values from -4 to 4, as said below
- x_line_class: int32 [256], P('gy'), may hold values from 0 to 3
- y_line_class: int32 [256], P('gx'), may hold values from 0 to 3
- box_offset: int32 [3, 2], replicated, may hold values from 0 to 63, as said below
- coupling: float32 [3, 3, 3], replicated, may hold values from -3 to 3
Outputs:
- fields_next: float32 [4, 3, 256, 8192], P('sec', None, 'gx', 'gy')
The draws below stay inside these ranges and needn't reach their ends.
Inputs may be any that keep to these rules, and one draw needn't show every extreme that they name: `box_offset`: column 0 is below 16 and column 1 below 64; each column reaches its largest value for some box. `x_ops`: A dense matrix for each class and characteristic. `y_ops`: A dense matrix for each class and characteristic.
All inputs are finite; a program needn't handle non-finite values.
Results may differ from the reference program's by a relative error of at most 0.00013.
Values sent between devices are 32-bit elements; how exact they have to be, the bound alone decides.
A program may use at most 64 MiB of HBM per device.

```python
import jax
import jax.numpy as jnp
from jax import lax

NX = 256
NY = 256
CZ = 32
NCLASS = 4
STEPS = 2
NBOX = 3
CX = 16
CY = 64
N_SEC = 4


def line_operators(key, length):
    subkeys = jax.random.split(key, 3)
    positions = jnp.arange(length)
    offset = positions[:, None] - positions[None, :]
    implicit_side = jnp.where(offset == 0, 1.0, jnp.where(jnp.abs(offset) == 1, 1.0 / 3.0, 0.0))
    explicit_side = 7.0 / 9.0 * ((offset == -1).astype(jnp.float32) - (offset == 1).astype(jnp.float32)) + 1.0 / 36.0 * ((offset == -2).astype(jnp.float32) - (offset == 2).astype(jnp.float32))
    derivative = jnp.linalg.solve(implicit_side, explicit_side)
    courant = jnp.exp(jax.random.uniform(subkeys[0], (NCLASS, 3, 1, 1), minval=jnp.log(96.0), maxval=jnp.log(256.0)))
    damping = jax.random.uniform(subkeys[1], (NCLASS, 3, length), minval=0.0, maxval=0.3)
    identity = jnp.eye(length, dtype=jnp.float32)
    system = identity * (1.0 + damping)[..., None] + courant * derivative
    explicit = jnp.broadcast_to(identity - courant * derivative, system.shape)
    compact = jnp.linalg.solve(system, explicit)
    scatter_part = jax.random.truncated_normal(subkeys[2], -3.0, 3.0, (NCLASS, 3, length, length), dtype=jnp.float32)
    coupled = compact + 0.15 / jnp.sqrt(jnp.float32(length)) * scatter_part
    return coupled.astype(jnp.float32)


def draw_x_ops(key, part):
    return line_operators(jax.random.fold_in(key, 11), NX)


def draw_y_ops(key, part):
    return line_operators(jax.random.fold_in(key, 23), NY)


def draw_box_offset(key, part):
    subkeys = jax.random.split(jax.random.fold_in(key, 37), 4)
    column_x = jax.random.randint(subkeys[0], (NBOX,), 0, CX)
    column_y = jax.random.randint(subkeys[1], (NBOX,), 0, CY)
    pick_x = jax.random.randint(subkeys[2], (), 0, NBOX)
    pick_y = jax.random.randint(subkeys[3], (), 0, NBOX)
    members = jnp.arange(NBOX)
    column_x = jnp.where(members == pick_x, CX - 1, column_x)
    column_y = jnp.where(members == pick_y, CY - 1, column_y)
    return jnp.stack([column_x, column_y], axis=1).astype(jnp.int32)


def touch_ends(drawn, rng, low, largest):
    longest = drawn.shape.index(max(drawn.shape))
    spots = []
    for shift in (0, 1):
        where = [jax.random.randint(jax.random.fold_in(rng, axis), (), 0, length) for axis, length in enumerate(drawn.shape)]
        where[longest] = (where[longest] + shift) % drawn.shape[longest]
        spots.append(tuple(where))
    return drawn.at[spots[0]].set(low).at[spots[1]].set(largest)


def block_levels(rng, shape, pieces, low, top_value):
    factor_of, own = 1.0, jax.random.fold_in(rng, 6)
    for dim, shards_of in pieces:
        heights = jnp.exp(jax.random.uniform(jax.random.fold_in(own, dim), (shards_of,), jnp.float32, low / len(pieces), top_value / len(pieces)))
        factor_of = factor_of * jnp.repeat(heights, shape[dim] // shards_of).reshape([-1 if axis == dim else 1 for axis in range(len(shape))])
    return factor_of


def gaussian(rng, extent, deviation, reach, cuts=(), kind=jnp.bfloat16):
    values = jax.random.normal(rng, extent, jnp.float32) * deviation
    if len(cuts) > 0:
        values = block_levels(rng, extent, cuts, -0.22, 0.18) * values
    return jnp.clip(values, min=-reach, max=reach).astype(kind)


def setup_inputs(seed: int = 0) -> dict:
    splits = jax.random.split(jax.random.key(seed), 8)
    return {
        "fields": gaussian(splits[0], (N_SEC, 3, NX, NY * CZ), 1.0, 6.0, ((0, 4), (2, 16), (3, 4)), jnp.float32),
        "x_ops": draw_x_ops(jax.random.fold_in(splits[7], 71), 0),
        "y_ops": draw_y_ops(jax.random.fold_in(splits[7], 71), 0),
        "x_line_class": touch_ends(jax.random.randint(splits[3], (NY,), 0, NCLASS), jax.random.fold_in(splits[3], 1), 0, NCLASS - 1).astype(jnp.int32),
        "y_line_class": touch_ends(jax.random.randint(splits[4], (NX,), 0, NCLASS), jax.random.fold_in(splits[4], 1), 0, NCLASS - 1).astype(jnp.int32),
        "box_offset": draw_box_offset(jax.random.fold_in(splits[7], 71), 0),
        "coupling": gaussian(splits[6], (NBOX, 3, 3), 0.6, 3.0, (), jnp.float32),
    }


time_step = 0.2
viscosity = 0.25
highest = lax.Precision.HIGHEST

def flow_core(padded):
    centre = padded[:, 1:-1, 1:-1, :]
    ahead_x = padded[:, 2:, 1:-1, :]
    behind_x = padded[:, :-2, 1:-1, :]
    ahead_y = padded[:, 1:-1, 2:, :]
    behind_y = padded[:, 1:-1, :-2, :]
    ahead_z = jnp.roll(centre, -1, axis=3)
    behind_z = jnp.roll(centre, 1, axis=3)
    slope_x = 0.5 * (ahead_x - behind_x)
    slope_y = 0.5 * (ahead_y - behind_y)
    slope_z = 0.5 * (ahead_z - behind_z)
    laplace = ahead_x + behind_x + ahead_y + behind_y + ahead_z + behind_z - 6.0 * centre
    omega_x = slope_y[2] - slope_z[1]
    omega_y = slope_z[0] - slope_x[2]
    omega_z = slope_x[1] - slope_y[0]
    lamb_vector = jnp.stack([omega_y * centre[2] - omega_z * centre[1], omega_z * centre[0] - omega_x * centre[2], omega_x * centre[1] - omega_y * centre[0]])
    updated = centre + time_step * (viscosity * laplace - lamb_vector)
    return (updated, lamb_vector)

def place_source(padded_lamb, offset_x, offset_y, matrix, span_x, span_y, extent_x, extent_y):
    anchor = jnp.zeros((), jnp.int32)
    corner_x = (span_x - offset_x - 1).astype(jnp.int32)
    corner_y = (span_y - offset_y - 1).astype(jnp.int32)
    window = lax.dynamic_slice(padded_lamb, (anchor, corner_x, corner_y, anchor), (3, extent_x + 1, extent_y + 1, padded_lamb.shape[3]))
    averaged = 0.25 * (window[:, :-1, :-1] + window[:, 1:, :-1] + window[:, :-1, 1:] + window[:, 1:, 1:])
    return jnp.einsum('kj,jxyz->kxyz', matrix, averaged, precision=highest)

def sweep_x(amplitudes, x_ops, x_line_class):
    result = jnp.zeros_like(amplitudes)
    for category in range(NCLASS):
        partial_value = jnp.einsum('kij,kjyz->kiyz', x_ops[category], amplitudes, precision=highest)
        chosen = (x_line_class == category).astype(jnp.float32)
        result = result + partial_value * chosen[None, None, :, None]
    return result

def sweep_y(amplitudes, y_ops, y_line_class):
    result = jnp.zeros_like(amplitudes)
    for category in range(NCLASS):
        partial_value = jnp.einsum('kij,kxjz->kxiz', y_ops[category], amplitudes, precision=highest)
        chosen = (y_line_class == category).astype(jnp.float32)
        result = result + partial_value * chosen[None, :, None, None]
    return result

def reference(fields, x_ops, y_ops, x_line_class, y_line_class, box_offset, coupling):
    arrays = fields.reshape(N_SEC, 3, NX, NY, CZ)
    velocities = [arrays[member] for member in range(NBOX)]
    amplitudes = arrays[NBOX]
    for repeat in range(STEPS):
        source_sum = jnp.zeros_like(amplitudes)
        for member in range(NBOX):
            padded = jnp.pad(velocities[member], ((0, 0), (1, 1), (1, 1), (0, 0)))
            updated, lamb_vector = flow_core(padded)
            stretched = jnp.pad(lamb_vector, ((0, 0), (CX, 0), (CY, 0), (0, 0)))
            source_sum = source_sum + place_source(stretched, box_offset[member, 0], box_offset[member, 1], coupling[member], CX, CY, NX, NY)
            velocities[member] = updated
        amplitudes = amplitudes + time_step * source_sum
        amplitudes = sweep_y(sweep_x(amplitudes, x_ops, x_line_class), y_ops, y_line_class)
    return jnp.stack(velocities + [amplitudes]).reshape(N_SEC, 3, NX, NY * CZ)
```

```python
import functools

import jax
import jax.numpy as jnp
from jax import lax
from jax.experimental import pallas as pl
from jax.experimental.pallas import tpu as pltpu
from jax.sharding import PartitionSpec as P

CZ = 32
NCLASS = 4
time_step = 0.2
viscosity = 0.25
MESH = pl.DeviceIdType.MESH
F32 = jnp.float32
BF16 = jnp.bfloat16

DIRS = [(dx, dy) for dx in (-1, 0, 1) for dy in (-1, 0, 1) if (dx, dy) != (0, 0)]


def owner_of(k, q):
    z = (3 * k + 1 + 4 * (q % 2)) % 8
    return 2 * (z // 4) + 1, (z % 4) * 4 + q % 4, q // 4


def roll(value, shift, axis):
    size = value.shape[axis]
    shift = shift % size
    return value if shift == 0 else pltpu.roll(value, shift, axis)


def lanes_of(value):
    return lax.broadcasted_iota(jnp.int32, value.shape, value.ndim - 1)


def swap_blocks(blocks):
    lane = lanes_of(blocks[0])
    blocks = list(blocks)
    for bit in (3, 2, 1, 0):
        d, width = 1 << bit, 2 << bit
        upper = (lane & width) != 0
        for i in range(16):
            if i & d:
                continue
            a, b = blocks[i], blocks[i | d]
            blocks[i] = jnp.where(upper, roll(b, width, 1), a)
            blocks[i | d] = jnp.where(upper, b, roll(a, -width, 1))
    return blocks


def take_lanes(value, index):
    return jnp.take_along_axis(value, index, axis=1, mode="promise_in_bounds")


def to_planes(blocks):
    lane = lanes_of(blocks[0])
    rest = lane % 64
    index = (rest % 4) * 32 + (rest // 4) * 2 + lane // 64
    return [take_lanes(b, index) for b in swap_blocks(blocks)]


def from_planes(blocks):
    lane = lanes_of(blocks[0])
    index = (lane % 2) * 64 + ((lane % 32) // 2) * 4 + lane // 32
    return swap_blocks([take_lanes(b, index) for b in blocks])


def pair_swap(a, b):
    upper = lanes_of(a) >= 64
    return jnp.where(upper, roll(b, 64, 1), a), jnp.where(upper, b, roll(a, 64, 1))


def split(value):
    high = value.astype(BF16)
    return high, (value - high.astype(F32)).astype(BF16)


def dot(a, b):
    return lax.dot_general(a, b, (((1,), (0,)), ((), ())), preferred_element_type=F32)


def flow_block(ref, j, lane):
    def block(c, at):
        return ref[c, :, pl.ds(pl.multiple_of(at * 128, 128), 128)]

    z = lane % CZ
    centre, ax, bx, ay, by, az, bz = [], [], [], [], [], [], []
    for c in range(3):
        cur, prv, nxt = block(c, j), block(c, j - 1), block(c, j + 1)
        centre.append(cur)
        ax.append(roll(cur, -1, 0))
        bx.append(roll(cur, 1, 0))
        ay.append(jnp.where(lane < 96, roll(cur, -32, 1), roll(nxt, -32, 1)))
        by.append(jnp.where(lane >= 32, roll(cur, 32, 1), roll(prv, 32, 1)))
        az.append(jnp.where(z != CZ - 1, roll(cur, -1, 1), roll(cur, 31, 1)))
        bz.append(jnp.where(z != 0, roll(cur, 1, 1), roll(cur, -31, 1)))
    omega_x = 0.5 * ((ay[2] - by[2]) - (az[1] - bz[1]))
    omega_y = 0.5 * ((az[0] - bz[0]) - (ax[2] - bx[2]))
    omega_z = 0.5 * ((ax[1] - bx[1]) - (ay[0] - by[0]))
    u, v, w = centre
    lamb = [omega_y * w - omega_z * v, omega_z * u - omega_x * w, omega_x * v - omega_y * u]
    updated = []
    for c in range(3):
        laplace = ax[c] + bx[c] + ay[c] + by[c] + az[c] + bz[c] - 6.0 * centre[c]
        updated.append(centre[c] + time_step * (viscosity * laplace - lamb[c]))
    return updated, lamb


def kernel(
    coup, off, f, xo, yo, cyl, cxl, out,
    U, V, M, hxs, hxr, hyr, cs, cr, PB, A, L, X, Y, CY, CX, R, Q,
    XH, XL, YH, YL, SX, SY, TH, TL, AH, AL, BH, BL,
    hss, hrs, pss, ars, lrs, xss, yss, css, dss, xrs, yrs, crs, drs, rss, rrs,
):
    sec, gx, gy = lax.axis_index("sec"), lax.axis_index("gx"), lax.axis_index("gy")
    is_flow = sec < 3
    my_q = gy * 4 + gx % 4
    my_z = (sec // 2) * 4 + gx // 4
    my_t = (my_z + 15 - 4 * (my_q % 2)) % 8
    is_owner = (sec % 2 == 1) & (my_t % 3 == 0)
    my_k = my_t // 3

    def remote(src, dst, ss, rs, device):
        return pltpu.make_async_remote_copy(
            src_ref=src, dst_ref=dst, send_sem=ss, recv_sem=rs, device_id=device, device_id_type=MESH
        )

    def inside(dx, dy):
        return (gx + dx >= 0) & (gx + dx < 16) & (gy + dy >= 0) & (gy + dy < 4)

    def halo_copy(n):
        dx, dy = DIRS[n]
        back = DIRS.index((-dx, -dy))
        device = (sec, gx + dx, gy + dy)
        if dy == 0:
            side = 0 if dx > 0 else 1
            return remote(hxs.at[side], hxr.at[side], hss.at[n], hrs.at[back], device)
        if dx == 0:
            side = 0 if dy > 0 else 1
            lanes = pl.ds(1920, 128) if dy > 0 else pl.ds(0, 128)
            return remote(f.at[:, :, lanes], hyr.at[side], hss.at[n], hrs.at[back], device)
        return remote(cs.at[n], cr.at[back], hss.at[n], hrs.at[back], device)

    @pl.when(is_flow)
    def _():
        for c in range(3):
            for side, rows in ((0, 14), (1, 0)):
                for part in range(4):
                    hxs[side, c, 2 * part:2 * part + 2, :] = f[c, rows:rows + 2, 512 * part:512 * part + 512]
        for n, (dx, dy) in enumerate(DIRS):
            if dx and dy:
                rows, lanes = (14 if dx > 0 else 0), (1920 if dy > 0 else 0)
                for c in range(3):
                    cs[n, 2 * c:2 * c + 2, :] = f[c, rows:rows + 2, lanes:lanes + 128]
        for n, (dx, dy) in enumerate(DIRS):
            @pl.when(inside(dx, dy))
            def _():
                halo_copy(n).start()

    rotation = 3 * gx + 12 * gy

    def each_piece(body):
        def step(i, carry):
            o = (i + rotation) % 48
            k, q = o // 16, o % 16
            osec, ogx, ogy = owner_of(k, q)
            mine = (osec == sec) & (ogx == gx) & (ogy == gy)
            body(o, k, q, (osec, ogx, ogy), mine)
            return carry

        lax.fori_loop(0, 48, step, 0)

    rows16, lanes128 = pl.ds(gx * 16, 16), pl.ds(gy * 128, 128)

    def send_pieces(t, target, recv):
        def body(o, k, q, device, mine):
            @pl.when(jnp.logical_not(mine))
            def _():
                remote(PB.at[t, k, q], target, pss.at[t, o], recv, device).start()

            @pl.when(mine)
            def _():
                pltpu.make_async_copy(PB.at[t, k, q], target, recv).start()

        each_piece(body)

    def drain_pieces(t, target, recv):
        def body(o, k, q, device, mine):
            @pl.when(jnp.logical_not(mine))
            def _():
                remote(PB.at[t, k, q], target, pss.at[t, o], recv, device).wait_send()

        each_piece(body)

    def planes_of(src, t):
        def body(k, carry):
            blocks = to_planes([src[k, :, 128 * g:128 * g + 128] for g in range(16)])
            for q in range(16):
                PB[t, k, q] = blocks[q]
            return carry

        lax.fori_loop(0, 3, body, 0)

    @pl.when(sec == 3)
    def _():
        planes_of(f, 0)
        send_pieces(0, A.at[rows16, lanes128], ars)

    def each_operator(body):
        for j in range(4):
            for k in range(3):
                osec, ogx, ogy = owner_of(k, gy * 4 + j)
                body(0, 3 * j + k, k, (osec == sec), (ogx == gx), (sec, ogx, gy))
                osec, ogx, ogy = owner_of(k, 4 * j + gx % 4)
                body(1, 3 * j + k, k, (osec == sec) & (ogx == gx), (gy == j), (sec, gx, j))

    def operator_copies(kind, n, k):
        if kind == 0:
            return (
                (xo.at[:, k], X.at[:, rows16], xss.at[n], xrs),
                (cyl, CY.at[rows16], css.at[n], crs),
            )
        return (
            (yo.at[:, k], Y.at[:, pl.ds(gy * 64, 64)], yss.at[n], yrs),
            (cxl, CX.at[:, lanes128], dss.at[n], drs),
        )

    def start_operator(kind, n, k, wanted, mine, device):
        @pl.when(wanted & jnp.logical_not(mine))
        def _():
            for src, dst, ss, rs in operator_copies(kind, n, k):
                remote(src, dst, ss, rs, device).start()

        @pl.when(wanted & mine)
        def _():
            for src, dst, ss, rs in operator_copies(kind, n, k):
                pltpu.make_async_copy(src, dst, rs).start()

    def drain_operator(kind, n, k, wanted, mine, device):
        @pl.when(wanted & jnp.logical_not(mine))
        def _():
            for src, dst, ss, rs in operator_copies(kind, n, k):
                remote(src, dst, ss, rs, device).wait_send()

    @pl.when(sec % 2 == 1)
    def _():
        each_operator(start_operator)

    lane = lax.broadcasted_iota(jnp.int32, (24, 128), 1)
    row = lax.broadcasted_iota(jnp.int32, (24, 128), 0)

    def mixed(lamb, k):
        return coup[k, 0] * lamb[0] + coup[k, 1] * lamb[1] + coup[k, 2] * lamb[2]

    def tile_rows(value):
        return roll(value, -2, 0)[:16]

    @pl.when(is_flow)
    def _():
        U[...] = jnp.zeros_like(U)
        for c in range(3):
            for g in range(16):
                U[c, 2:18, 256 + 128 * g:384 + 128 * g] = f[c, :, 128 * g:128 * g + 128]
        for n, (dx, dy) in enumerate(DIRS):
            rows = {-1: 0, 0: 2, 1: 18}[dx]
            lanes = {-1: 128, 0: 256, 1: 2304}[dy]

            @pl.when(inside(dx, dy))
            def _():
                if dy == 0:
                    side = 0 if dx < 0 else 1
                    pltpu.make_async_copy(hxr.at[side], hxr.at[side], hrs.at[n]).wait()
                    for c in range(3):
                        for part in range(4):
                            U[c, rows:rows + 2, lanes + 512 * part:lanes + 512 * part + 512] = hxr[side, c, 2 * part:2 * part + 2, :]
                elif dx == 0:
                    side = 0 if dy < 0 else 1
                    pltpu.make_async_copy(hyr.at[side], hyr.at[side], hrs.at[n]).wait()
                    for c in range(3):
                        U[c, 2:18, lanes:lanes + 128] = hyr[side, c]
                else:
                    pltpu.make_async_copy(cr.at[n], cr.at[n], hrs.at[n]).wait()
                    for c in range(3):
                        U[c, rows:rows + 2, lanes:lanes + 128] = cr[n, 2 * c:2 * c + 2, :]

        V[...] = jnp.zeros_like(V)
        valid = ((row >= 2) | (gx > 0)) & ((row < 18) | (gx < 15))

        def edge(j, there):
            updated, _ = flow_block(U, j, lane)
            for c in range(3):
                V[c, :, 128 * j:128 * j + 128] = jnp.where(valid & there, updated[c], 0.0)

        edge(1, gy > 0)
        edge(18, gy < 3)

        def first(j, carry):
            updated, lamb = flow_block(U, j, lane)
            for c in range(3):
                V[c, :, pl.ds(pl.multiple_of(j * 128, 128), 128)] = jnp.where(valid, updated[c], 0.0)
                M[c, :, pl.ds(pl.multiple_of((j - 2) * 128, 128), 128)] = tile_rows(mixed(lamb, c))
            return carry

        lax.fori_loop(2, 18, first, 0)
        planes_of(M, 0)
        send_pieces(0, L.at[0, sec, rows16, lanes128], lrs.at[0])

        def second(j, carry):
            updated, lamb = flow_block(V, j, lane)
            for c in range(3):
                at = pl.ds(pl.multiple_of((j - 2) * 128, 128), 128)
                out[c, :, at] = tile_rows(updated[c])
                M[c, :, at] = tile_rows(mixed(lamb, c))
            return carry

        lax.fori_loop(2, 18, second, 0)
        planes_of(M, 1)
        send_pieces(1, L.at[1, sec, rows16, lanes128], lrs.at[1])

    @pl.when(is_owner)
    def _():
        i = lax.broadcasted_iota(jnp.int32, (256, 256), 0)
        j = lax.broadcasted_iota(jnp.int32, (256, 256), 1)
        for s in range(3):
            d = i - j - off[s, 0]
            SX[s] = jnp.where((d == 0) | (d == 1), 0.5, 0.0).astype(BF16)
            d = j - i - off[s, 1]
            SY[s] = jnp.where((d == 0) | (d == 1), 0.5, 0.0).astype(BF16)
        for ref, sem in ((X, xrs), (Y, yrs), (CY, crs), (CX, drs)):
            pltpu.make_async_copy(ref, ref, sem).wait()
        for c in range(NCLASS):
            high, low = split(X[c])
            XH[:, 256 * c:256 * c + 256] = high
            XL[:, 256 * c:256 * c + 256] = low
            high, low = split(Y[c].T)
            YH[256 * c:256 * c + 256, :] = high
            YL[256 * c:256 * c + 256, :] = low

        def separated(ref):
            a0, b0 = pair_swap(ref[:, 0:128], ref[:, 128:256])
            a1, b1 = pair_swap(ref[:, 256:384], ref[:, 384:512])
            return jnp.concatenate([a0, a1], axis=1), jnp.concatenate([b0, b1], axis=1)

        column_class = separated(CX)[0][0:1, :]
        column_class = jnp.concatenate([column_class, column_class], axis=1)
        row_class = CY[:, 0:1]

        def add_source(t):
            for s in range(3):
                for z, plane in enumerate(separated(L.at[t, s])):
                    high, low = split(plane)
                    shifted = dot(high, SY[s]) + dot(low, SY[s])
                    high, low = split(shifted)
                    TH[256 * s:256 * s + 256, 256 * z:256 * z + 256] = high
                    TL[256 * s:256 * s + 256, 256 * z:256 * z + 256] = low
            total = R[...]
            for s in range(3):
                total += dot(SX[s], TH[256 * s:256 * s + 256, :]) + dot(SX[s], TL[256 * s:256 * s + 256, :])
            return total

        def sweeps(value):
            high, low = split(value)
            for c in range(NCLASS):
                keep = column_class == c
                AH[256 * c:256 * c + 256, :] = jnp.where(keep, high, jnp.zeros_like(high))
                AL[256 * c:256 * c + 256, :] = jnp.where(keep, low, jnp.zeros_like(low))
            swept = dot(XH[...], AH[...]) + dot(XL[...], AH[...]) + dot(XH[...], AL[...])
            high, low = split(swept)
            for c in range(NCLASS):
                keep = row_class == c
                for z in range(2):
                    part_h, part_l = high[:, 256 * z:256 * z + 256], low[:, 256 * z:256 * z + 256]
                    BH[256 * z:256 * z + 256, 256 * c:256 * c + 256] = jnp.where(keep, part_h, jnp.zeros_like(part_h))
                    BL[256 * z:256 * z + 256, 256 * c:256 * c + 256] = jnp.where(keep, part_l, jnp.zeros_like(part_l))
            return dot(BH[...], YH[...]) + dot(BL[...], YH[...]) + dot(BH[...], YL[...])

        pltpu.make_async_copy(A, A, ars).wait()
        p0, p1 = separated(A)
        R[:, 0:256], R[:, 256:512] = p0, p1
        pltpu.make_async_copy(L.at[0], L.at[0], lrs.at[0]).wait()
        result = sweeps(add_source(0))
        R[:, 0:256], R[:, 256:512] = result[0:256], result[256:512]
        pltpu.make_async_copy(L.at[1], L.at[1], lrs.at[1]).wait()
        result = sweeps(add_source(1))
        for h in range(2):
            a, b = pair_swap(result[0:256, 128 * h:128 * h + 128], result[256:512, 128 * h:128 * h + 128])
            R[:, 256 * h:256 * h + 128] = a
            R[:, 256 * h + 128:256 * h + 256] = b

        def back(n):
            tx, ty = n % 16, n // 16
            mine = (sec == 3) & (tx == gx) & (ty == gy)
            src = R.at[pl.ds(pl.multiple_of(tx * 16, 16), 16), pl.ds(pl.multiple_of(ty * 128, 128), 128)]
            return mine, src, Q.at[my_k, my_q], (3, tx, ty)

        def give(i, carry):
            n = (i + rotation) % 64
            mine, src, dst, device = back(n)

            @pl.when(jnp.logical_not(mine))
            def _():
                remote(src, dst, rss.at[n], rrs, device).start()

            @pl.when(mine)
            def _():
                pltpu.make_async_copy(src, dst, rrs).start()

            return carry

        lax.fori_loop(0, 64, give, 0)

        def drain(n, carry):
            mine, src, dst, device = back(n)

            @pl.when(jnp.logical_not(mine))
            def _():
                remote(src, dst, rss.at[n], rrs, device).wait_send()

            return carry

        lax.fori_loop(0, 64, drain, 0)

    @pl.when(sec == 3)
    def _():
        pltpu.make_async_copy(Q, Q, rrs).wait()

        def body(k, carry):
            blocks = from_planes([Q[k, q] for q in range(16)])
            for g in range(16):
                out[k, :, 128 * g:128 * g + 128] = blocks[g]
            return carry

        lax.fori_loop(0, 3, body, 0)
        drain_pieces(0, A.at[rows16, lanes128], ars)

    @pl.when(sec % 2 == 1)
    def _():
        each_operator(drain_operator)

    @pl.when(is_flow)
    def _():
        for n, (dx, dy) in enumerate(DIRS):
            @pl.when(inside(dx, dy))
            def _():
                halo_copy(n).wait_send()
        for t in range(2):
            drain_pieces(t, L.at[t, sec, rows16, lanes128], lrs.at[t])


def local(fields, x_ops, y_ops, x_line_class, y_line_class, box_offset, coupling):
    member = jnp.minimum(lax.axis_index("sec"), 2)
    matrix = time_step * lax.dynamic_index_in_dim(coupling, member, 0, keepdims=False)
    row_class = jnp.broadcast_to(y_line_class.astype(F32)[:, None], (16, 128))
    column_class = jnp.broadcast_to(jnp.tile(x_line_class.astype(F32), 2)[None, :], (8, 128))
    vmem, smem, any_space = (pl.BlockSpec(memory_space=m) for m in (pltpu.VMEM, pltpu.SMEM, pl.ANY))
    V, D = pltpu.VMEM, pltpu.SemaphoreType.DMA
    out = pl.pallas_call(
        kernel,
        out_shape=jax.ShapeDtypeStruct((3, 16, 2048), F32),
        in_specs=[smem, smem, vmem, any_space, any_space, vmem, vmem],
        out_specs=vmem,
        scratch_shapes=[
            V((3, 24, 2560), F32), V((3, 24, 2560), F32), V((3, 16, 2048), F32),
            V((2, 3, 8, 512), F32), V((2, 3, 8, 512), F32), V((2, 3, 16, 128), F32),
            V((8, 8, 128), F32), V((8, 8, 128), F32),
            V((2, 3, 16, 16, 128), F32), V((256, 512), F32), V((2, 3, 256, 512), F32),
            V((4, 256, 256), F32), V((4, 256, 256), F32), V((256, 128), F32), V((8, 512), F32),
            V((256, 512), F32), V((3, 16, 16, 128), F32),
            V((256, 1024), BF16), V((256, 1024), BF16), V((1024, 256), BF16), V((1024, 256), BF16),
            V((3, 256, 256), BF16), V((3, 256, 256), BF16), V((768, 512), BF16), V((768, 512), BF16),
            V((1024, 512), BF16), V((1024, 512), BF16), V((512, 1024), BF16), V((512, 1024), BF16),
            D((8,)), D((8,)), D((2, 48)), D, D((2,)),
            D((12,)), D((12,)), D((12,)), D((12,)), D, D, D, D, D((64,)), D,
        ],
        compiler_params=pltpu.CompilerParams(has_side_effects=True, vmem_limit_bytes=60 << 20),
    )(matrix, box_offset, fields[0], x_ops, y_ops, row_class, column_class)
    return out[None]


def solution(mesh):
    placed = (
        P("sec", None, "gx", "gy"),
        P(None, None, "gx", None),
        P(None, None, "gy", None),
        P("gy"),
        P("gx"),
        P(),
        P(),
    )
    return jax.shard_map(
        local, mesh=mesh, in_specs=placed, out_specs=P("sec", None, "gx", "gy"), check_vma=False
    )
```

```python
import functools

import jax
import jax.numpy as jnp
from jax import lax
from jax.experimental import pallas as pl
from jax.experimental.pallas import tpu as pltpu
from jax.sharding import PartitionSpec as P

CZ = 32
NCLASS = 4
time_step = 0.2
viscosity = 0.25
MESH = pl.DeviceIdType.MESH
F32 = jnp.float32
BF16 = jnp.bfloat16

DIRS = [(dx, dy) for dx in (-1, 0, 1) for dy in (-1, 0, 1) if (dx, dy) != (0, 0)]


def div(a, b):
    return lax.div(a, jnp.int32(b))


def rem(a, b):
    return lax.rem(a, jnp.int32(b))


def device_at(x, y, z, core):
    return 2 * div(z, 4) + core, rem(z, 4) * 4 + y, x


def owner_of(m, q):
    z = m + (m >= 4).astype(jnp.int32)
    return device_at(div(q, 4), rem(q, 4), z, 1)


def roll(value, shift, axis):
    size = value.shape[axis]
    shift = shift % size
    return value if shift == 0 else pltpu.roll(value, shift, axis)


def lanes_of(value):
    return lax.broadcasted_iota(jnp.int32, value.shape, value.ndim - 1)


def swap_blocks(blocks):
    lane = lanes_of(blocks[0])
    blocks = list(blocks)
    for bit in (3, 2, 1, 0):
        d, width = 1 << bit, 2 << bit
        upper = (lane & width) != 0
        for i in range(16):
            if i & d:
                continue
            a, b = blocks[i], blocks[i | d]
            blocks[i] = jnp.where(upper, roll(b, width, 1), a)
            blocks[i | d] = jnp.where(upper, b, roll(a, -width, 1))
    return blocks


def take_lanes(value, index):
    return jnp.take_along_axis(value, index, axis=1, mode="promise_in_bounds")


def to_planes(blocks):
    lane = lanes_of(blocks[0])
    rest = lane % 64
    index = (rest % 4) * 32 + (rest // 4) * 2 + lane // 64
    return [take_lanes(b, index) for b in swap_blocks(blocks)]


def from_planes(blocks):
    lane = lanes_of(blocks[0])
    index = (lane % 2) * 64 + ((lane % 32) // 2) * 4 + lane // 32
    return swap_blocks([take_lanes(b, index) for b in blocks])


def pair_swap(a, b):
    upper = lanes_of(a) >= 64
    return jnp.where(upper, roll(b, 64, 1), a), jnp.where(upper, b, roll(a, 64, 1))


def split(value):
    high = value.astype(BF16)
    return high, (value - high.astype(F32)).astype(BF16)


def dot(a, b):
    return lax.dot_general(a, b, (((1,), (0,)), ((), ())), preferred_element_type=F32)


def flow_block(ref, j, lane):
    def block(c, at):
        return ref[c, :, pl.ds(pl.multiple_of(at * 128, 128), 128)]

    z = lane % CZ
    centre, ax, bx, ay, by, az, bz = [], [], [], [], [], [], []
    for c in range(3):
        cur, prv, nxt = block(c, j), block(c, j - 1), block(c, j + 1)
        centre.append(cur)
        ax.append(roll(cur, -1, 0))
        bx.append(roll(cur, 1, 0))
        ay.append(jnp.where(lane < 96, roll(cur, -32, 1), roll(nxt, -32, 1)))
        by.append(jnp.where(lane >= 32, roll(cur, 32, 1), roll(prv, 32, 1)))
        az.append(jnp.where(z != CZ - 1, roll(cur, -1, 1), roll(cur, 31, 1)))
        bz.append(jnp.where(z != 0, roll(cur, 1, 1), roll(cur, -31, 1)))
    omega_x = 0.5 * ((ay[2] - by[2]) - (az[1] - bz[1]))
    omega_y = 0.5 * ((az[0] - bz[0]) - (ax[2] - bx[2]))
    omega_z = 0.5 * ((ax[1] - bx[1]) - (ay[0] - by[0]))
    u, v, w = centre
    lamb = [omega_y * w - omega_z * v, omega_z * u - omega_x * w, omega_x * v - omega_y * u]
    updated = []
    for c in range(3):
        laplace = ax[c] + bx[c] + ay[c] + by[c] + az[c] + bz[c] - 6.0 * centre[c]
        updated.append(centre[c] + time_step * (viscosity * laplace - lamb[c]))
    return updated, lamb


def kernel(
    coup, off, f, xo, yo, xcls, ycls, out,
    U, V, M, hxs, hxr, hyr, cs, cr, PB, A, L, X, Y, CY, CX, CYL, CXL, R, D, Q,
    XH, XL, YH, YL, SX, SY, TH, TL, AH, AL, BH, BL,
    hss, hrs, pss, ars, lrs, xss, yss, css, dss, xrs, yrs, crs, drs, rss, rrs, known_x, known_y,
):
    sec, gx, gy = lax.axis_index("sec"), lax.axis_index("gx"), lax.axis_index("gy")
    x, y, z, core = gy, rem(gx, 4), 4 * div(sec, 2) + div(gx, 4), rem(sec, 2)
    is_flow = sec < 3
    is_owner = (core == 1) & (z != 4) & (z != 7)
    my_q = 4 * x + y
    my_m = z - (z > 4).astype(jnp.int32)
    my_o = my_m * 16 + my_q

    def remote(src, dst, ss, rs, device):
        return pltpu.make_async_remote_copy(
            src_ref=src, dst_ref=dst, send_sem=ss, recv_sem=rs, device_id=device, device_id_type=MESH
        )

    def wait_for(ref, sem):
        pltpu.make_async_copy(ref, ref, sem).wait()

    def signal(sem, device):
        pl.semaphore_signal(sem, inc=1, device_id=device, device_id_type=MESH)

    barrier = pltpu.get_barrier_semaphore()
    greeted = 0
    for dx, dy in DIRS:
        signal(barrier, (sec, rem(gx + dx + 16, 16), rem(gy + dy + 4, 4)))
        greeted += 1
    signal(barrier, device_at(rem(x + 2, 4), y, z, core))
    for d in (1, 2, 3):
        signal(barrier, device_at(x, rem(y + d, 4), z, core))
    signal(barrier, device_at(x, y, z, 1 - core))
    for d in range(1, 8):
        for c in range(2):
            signal(barrier, device_at(x, y, rem(z + d, 8), c))
    greeted += 1 + 3 + 1 + 14

    def inside(dx, dy):
        return (gx + dx >= 0) & (gx + dx < 16) & (gy + dy >= 0) & (gy + dy < 4)

    @pl.when(is_flow)
    def _():
        for c in range(3):
            for side, rows in ((0, 14), (1, 0)):
                for part in range(4):
                    hxs[side, c, 2 * part:2 * part + 2, :] = f[c, rows:rows + 2, 512 * part:512 * part + 512]
        for n, (dx, dy) in enumerate(DIRS):
            if dx and dy:
                rows, lanes = (14 if dx > 0 else 0), (1920 if dy > 0 else 0)
                for c in range(3):
                    cs[n, 2 * c:2 * c + 2, :] = f[c, rows:rows + 2, lanes:lanes + 128]
        U[...] = jnp.zeros_like(U)
        for c in range(3):
            for g in range(16):
                U[c, 2:18, 256 + 128 * g:384 + 128 * g] = f[c, :, 128 * g:128 * g + 128]
        for c in range(3):
            for j in (0, 1, 18, 19):
                V[c, :, 128 * j:128 * j + 128] = jnp.zeros((24, 128), F32)

    @pl.when(core == 1)
    def _():
        CXL[...] = jnp.zeros_like(CXL)
        CXL[:, 0:64] = jnp.broadcast_to(xcls[...].astype(F32), (8, 64))
        spread = jnp.broadcast_to(ycls[...].astype(F32), (16, 16))
        diagonal = lax.broadcasted_iota(jnp.int32, (16, 16), 0) == lax.broadcasted_iota(jnp.int32, (16, 16), 1)
        column = jnp.sum(jnp.where(diagonal, spread, 0.0), axis=1, keepdims=True)
        CYL[...] = jnp.broadcast_to(column, (16, 128))

    pl.semaphore_wait(barrier, greeted)

    def halo_copy(n):
        dx, dy = DIRS[n]
        back = DIRS.index((-dx, -dy))
        device = (sec, gx + dx, gy + dy)
        if dy == 0:
            side = 0 if dx > 0 else 1
            return remote(hxs.at[side], hxr.at[side], hss.at[n], hrs.at[back], device)
        if dx == 0:
            side = 0 if dy > 0 else 1
            lanes = pl.ds(1920, 128) if dy > 0 else pl.ds(0, 128)
            return remote(f.at[:, :, lanes], hyr.at[side], hss.at[n], hrs.at[back], device)
        return remote(cs.at[n], cr.at[back], hss.at[n], hrs.at[back], device)

    @pl.when(is_flow)
    def _():
        for n, (dx, dy) in enumerate(DIRS):
            @pl.when(inside(dx, dy))
            def _():
                halo_copy(n).start()

    for d in (1, 2, 3):
        signal(known_x, device_at(rem(x + d, 4), y, z, core))

    rotation = 16 * rem(z, 6) + my_q
    rows8, rows16, lanes128 = pl.ds(gx * 8, 8), pl.ds(gx * 16, 16), pl.ds(gy * 128, 128)

    def send_pieces(t, target, recv):
        def step(i, carry):
            o = i + rotation
            o = jnp.where(o >= 96, o - 96, o)
            device = owner_of(div(o, 16), rem(o, 16))
            mine = is_owner & (o == my_o)

            @pl.when(jnp.logical_not(mine))
            def _():
                remote(PB.at[t, o], target, pss.at[t], recv, device).start()

            @pl.when(mine)
            def _():
                pltpu.make_async_copy(PB.at[t, o], target, recv).start()

            return carry

        lax.fori_loop(0, 96, step, 0)

    def drain_pieces(t):
        @pl.when(is_owner)
        def _():
            wait_for(PB.at[t, pl.ds(0, 95)], pss.at[t])

        @pl.when(jnp.logical_not(is_owner))
        def _():
            wait_for(PB.at[t], pss.at[t])

    def planes_of(src, t):
        def body(k, carry):
            blocks = to_planes([src[k, :, 128 * g:128 * g + 128] for g in range(16)])
            for q in range(16):
                even, odd = pair_swap(blocks[q][0:8], blocks[q][8:16])
                PB[t, 32 * k + q] = even
                PB[t, 32 * k + 16 + q] = odd
            return carry

        lax.fori_loop(0, 3, body, 0)

    def each_operator(body):
        for dz in (-2, -1, 0, 1, 2):
            oz = rem(z + dz + 8, 8)
            k = div(oz - (oz > 4).astype(jnp.int32), 2)
            holds = (oz != 4) & (oz != 7)
            for j in range(4):
                wanted = holds
                if dz in (-2, 2):
                    wanted = holds & (rem(x + j, 2) == (0 if dz < 0 else 1))
                mine = (y == j) if dz == 0 else None
                body(0, 4 * (dz + 2) + j, k, wanted, mine, device_at(x, j, oz, 1))
        for j in range(4):
            body(1, j, div(my_m, 2), is_owner, x == j, device_at(j, y, z, 1))

    def operator_copies(kind, n, k):
        if kind == 0:
            return (
                (xo.at[:, k], X.at[:, rows16], xss.at[n], xrs),
                (CYL, CY.at[rows16], css.at[n], crs),
            )
        return (
            (yo.at[:, k], Y.at[:, pl.ds(gy * 64, 64)], yss.at[n], yrs),
            (CXL, CX.at[:, lanes128], dss.at[n], drs),
        )

    def start_operator(kind, n, k, wanted, mine, device):
        far = wanted if mine is None else wanted & jnp.logical_not(mine)

        @pl.when(far)
        def _():
            for src, dst, ss, rs in operator_copies(kind, n, k):
                remote(src, dst, ss, rs, device).start()

        if mine is not None:
            @pl.when(wanted & mine)
            def _():
                for src, dst, ss, rs in operator_copies(kind, n, k):
                    pltpu.make_async_copy(src, dst, rs).start()

    def drain_operator(kind, n, k, wanted, mine, device):
        far = wanted if mine is None else wanted & jnp.logical_not(mine)

        @pl.when(far)
        def _():
            for src, dst, ss, rs in operator_copies(kind, n, k):
                remote(src, dst, ss, rs, device).wait_send()

    @pl.when(sec == 3)
    def _():
        planes_of(f, 0)

    pl.semaphore_wait(known_x, 3)
    for d in (1, 2, 3):
        signal(known_y, device_at(x, rem(y + d, 4), z, core))

    lane = lax.broadcasted_iota(jnp.int32, (24, 128), 1)
    row = lax.broadcasted_iota(jnp.int32, (24, 128), 0)

    def mixed(lamb, k):
        at = jnp.minimum(sec, 2)
        total = coup[at, k, 0] * lamb[0] + coup[at, k, 1] * lamb[1] + coup[at, k, 2] * lamb[2]
        return time_step * total

    def tile_rows(value):
        return roll(value, -2, 0)[:16]

    @pl.when(is_flow)
    def _():
        for n, (dx, dy) in enumerate(DIRS):
            rows = {-1: 0, 0: 2, 1: 18}[dx]
            lanes = {-1: 128, 0: 256, 1: 2304}[dy]

            @pl.when(inside(dx, dy))
            def _():
                if dy == 0:
                    side = 0 if dx < 0 else 1
                    wait_for(hxr.at[side], hrs.at[n])
                    for c in range(3):
                        for part in range(4):
                            U[c, rows:rows + 2, lanes + 512 * part:lanes + 512 * part + 512] = hxr[side, c, 2 * part:2 * part + 2, :]
                elif dx == 0:
                    side = 0 if dy < 0 else 1
                    wait_for(hyr.at[side], hrs.at[n])
                    for c in range(3):
                        U[c, 2:18, lanes:lanes + 128] = hyr[side, c]
                else:
                    wait_for(cr.at[n], hrs.at[n])
                    for c in range(3):
                        U[c, rows:rows + 2, lanes:lanes + 128] = cr[n, 2 * c:2 * c + 2, :]

    pl.semaphore_wait(known_y, 3)

    @pl.when(core == 1)
    def _():
        each_operator(start_operator)

    @pl.when(sec == 3)
    def _():
        send_pieces(0, A.at[rows8, lanes128], ars)

    @pl.when(is_flow)
    def _():
        valid = ((row >= 2) | (gx > 0)) & ((row < 18) | (gx < 15))

        def edge(j, there):
            updated, _ = flow_block(U, j, lane)
            for c in range(3):
                V[c, :, 128 * j:128 * j + 128] = jnp.where(valid & there, updated[c], 0.0)

        def first(j, carry):
            updated, lamb = flow_block(U, j, lane)
            for c in range(3):
                V[c, :, pl.ds(pl.multiple_of(j * 128, 128), 128)] = jnp.where(valid, updated[c], 0.0)
                M[c, :, pl.ds(pl.multiple_of((j - 2) * 128, 128), 128)] = tile_rows(mixed(lamb, c))
            return carry

        lax.fori_loop(2, 18, first, 0)
        planes_of(M, 0)
        send_pieces(0, L.at[0, sec, rows8, lanes128], lrs.at[0])
        edge(1, gy > 0)
        edge(18, gy < 3)

        def second(j, carry):
            updated, lamb = flow_block(V, j, lane)
            for c in range(3):
                at = pl.ds(pl.multiple_of((j - 2) * 128, 128), 128)
                out[c, :, at] = tile_rows(updated[c])
                M[c, :, at] = tile_rows(mixed(lamb, c))
            return carry

        lax.fori_loop(2, 18, second, 0)
        planes_of(M, 1)
        send_pieces(1, L.at[1, sec, rows8, lanes128], lrs.at[1])

    @pl.when(is_owner)
    def _():
        i = lax.broadcasted_iota(jnp.int32, (256, 256), 0)
        j = lax.broadcasted_iota(jnp.int32, (256, 256), 1)
        for s in range(3):
            d = i - j - off[0, s]
            SX[:, 256 * s:256 * s + 256] = jnp.where((d == 0) | (d == 1), 0.5, 0.0).astype(BF16)
            d = j - i - off[1, s]
            SY[s] = jnp.where((d == 0) | (d == 1), 0.5, 0.0).astype(BF16)
        for ref, sem in ((X, xrs), (Y, yrs), (CY, crs), (CX, drs)):
            wait_for(ref, sem)
        for c in range(NCLASS):
            high, low = split(X[c])
            XH[:, 256 * c:256 * c + 256] = high
            XL[:, 256 * c:256 * c + 256] = low
            high, low = split(Y[c].T)
            YH[256 * c:256 * c + 256, :] = high
            YL[256 * c:256 * c + 256, :] = low

        def unpacked(ref):
            halves = []
            for h in range(2):
                a, b = pair_swap(ref[:, 256 * h:256 * h + 128], ref[:, 256 * h + 128:256 * h + 256])
                rows = jnp.stack([a.reshape(16, 8, 128), b.reshape(16, 8, 128)], axis=1)
                halves.append(rows.reshape(256, 128))
            return jnp.concatenate(halves, axis=1)

        column_class = jnp.concatenate(
            [pair_swap(CX[:, 256 * h:256 * h + 128], CX[:, 256 * h + 128:256 * h + 256])[0][0:1] for h in range(2)], axis=1
        )
        row_class = CY[:, 0:1]

        def add_source(t):
            for s in range(3):
                high, low = split(unpacked(L.at[t, s]))
                high, low = split(dot(high, SY[s]) + dot(low, SY[s]))
                TH[256 * s:256 * s + 256, :] = high
                TL[256 * s:256 * s + 256, :] = low
            return D[...] + dot(SX[...], TH[...]) + dot(SX[...], TL[...])

        def sweeps(value):
            high, low = split(value)
            for c in range(NCLASS):
                keep = column_class == c
                AH[256 * c:256 * c + 256, :] = jnp.where(keep, high, jnp.zeros_like(high))
                AL[256 * c:256 * c + 256, :] = jnp.where(keep, low, jnp.zeros_like(low))
            swept = dot(XH[...], AH[...]) + dot(XL[...], AH[...]) + dot(XH[...], AL[...])
            high, low = split(swept)
            for c in range(NCLASS):
                keep = row_class == c
                BH[:, 256 * c:256 * c + 256] = jnp.where(keep, high, jnp.zeros_like(high))
                BL[:, 256 * c:256 * c + 256] = jnp.where(keep, low, jnp.zeros_like(low))
            return dot(BH[...], YH[...]) + dot(BL[...], YH[...]) + dot(BH[...], YL[...])

        wait_for(A, ars)
        D[...] = unpacked(A)
        wait_for(L.at[0], lrs.at[0])
        D[...] = sweeps(add_source(0))
        wait_for(L.at[1], lrs.at[1])
        result = sweeps(add_source(1))
        for h in range(2):
            rows = result[:, 128 * h:128 * h + 128].reshape(16, 2, 8, 128)
            a, b = pair_swap(rows[:, 0].reshape(128, 128), rows[:, 1].reshape(128, 128))
            R[:, 256 * h:256 * h + 128] = a
            R[:, 256 * h + 128:256 * h + 256] = b

        def give(i, carry):
            n = i + 16 * y + 4 * x + rem(z, 4)
            n = jnp.where(n >= 64, n - 64, n)
            tx, ty = div(n, 4), rem(n, 4)
            mine = (sec == 3) & (tx == gx) & (ty == gy)
            src = R.at[pl.ds(pl.multiple_of(tx * 8, 8), 8), pl.ds(pl.multiple_of(ty * 128, 128), 128)]

            @pl.when(jnp.logical_not(mine))
            def _():
                remote(src, Q.at[my_o], rss, rrs, (3, tx, ty)).start()

            @pl.when(mine)
            def _():
                pltpu.make_async_copy(src, Q.at[my_o], rrs).start()

            return carry

        lax.fori_loop(0, 64, give, 0)

    @pl.when(sec == 3)
    def _():
        wait_for(Q, rrs)

        def body(k, carry):
            blocks = []
            for q in range(16):
                a, b = pair_swap(Q[32 * k + q], Q[32 * k + 16 + q])
                blocks.append(jnp.concatenate([a, b], axis=0))
            blocks = from_planes(blocks)
            for g in range(16):
                out[k, :, 128 * g:128 * g + 128] = blocks[g]
            return carry

        lax.fori_loop(0, 3, body, 0)
        drain_pieces(0)

    @pl.when(is_owner & (sec == 3))
    def _():
        wait_for(Q.at[pl.ds(0, 63)], rss)

    @pl.when(is_owner & (sec != 3))
    def _():
        wait_for(Q.at[pl.ds(0, 64)], rss)

    @pl.when(core == 1)
    def _():
        each_operator(drain_operator)

    @pl.when(is_flow)
    def _():
        for n, (dx, dy) in enumerate(DIRS):
            @pl.when(inside(dx, dy))
            def _():
                halo_copy(n).wait_send()
        for t in range(2):
            drain_pieces(t)


def local(fields, x_ops, y_ops, x_line_class, y_line_class, box_offset, coupling):
    vmem, smem, any_space = (pl.BlockSpec(memory_space=m) for m in (pltpu.VMEM, pltpu.SMEM, pl.ANY))
    V, D = pltpu.VMEM, pltpu.SemaphoreType.DMA
    out = pl.pallas_call(
        kernel,
        out_shape=jax.ShapeDtypeStruct((3, 16, 2048), F32),
        in_specs=[smem, smem, vmem, any_space, any_space, vmem, vmem],
        out_specs=vmem,
        scratch_shapes=[
            V((3, 24, 2560), F32), V((3, 24, 2560), F32), V((3, 16, 2048), F32),
            V((2, 3, 8, 512), F32), V((2, 3, 8, 512), F32), V((2, 3, 16, 128), F32),
            V((8, 8, 128), F32), V((8, 8, 128), F32),
            V((2, 96, 8, 128), F32), V((128, 512), F32), V((2, 3, 128, 512), F32),
            V((4, 256, 256), F32), V((4, 256, 256), F32), V((256, 128), F32), V((8, 512), F32),
            V((16, 128), F32), V((8, 128), F32),
            V((128, 512), F32), V((256, 256), F32), V((96, 8, 128), F32),
            V((256, 1024), BF16), V((256, 1024), BF16), V((1024, 256), BF16), V((1024, 256), BF16),
            V((256, 768), BF16), V((3, 256, 256), BF16), V((768, 256), BF16), V((768, 256), BF16),
            V((1024, 256), BF16), V((1024, 256), BF16), V((256, 1024), BF16), V((256, 1024), BF16),
            D((8,)), D((8,)), D((2,)), D, D((2,)),
            D((20,)), D((4,)), D((20,)), D((4,)), D, D, D, D, D, D,
            pltpu.SemaphoreType.REGULAR, pltpu.SemaphoreType.REGULAR,
        ],
        compiler_params=pltpu.CompilerParams(
            collective_id=0, has_side_effects=True, vmem_limit_bytes=60 << 20
        ),
    )(coupling, box_offset.T, fields[0], x_ops, y_ops, x_line_class[None], y_line_class[None])
    return out[None]


def solution(mesh):
    placed = (
        P("sec", None, "gx", "gy"),
        P(None, None, "gx", None),
        P(None, None, "gy", None),
        P("gy"),
        P("gx"),
        P(),
        P(),
    )
    return jax.shard_map(
        local, mesh=mesh, in_specs=placed, out_specs=P("sec", None, "gx", "gy"), check_vma=False
    )
```

```python
import functools

import jax
import jax.numpy as jnp
from jax import lax
from jax.experimental import pallas as pl
from jax.experimental.pallas import tpu as pltpu
from jax.sharding import PartitionSpec as P

CZ = 32
NCLASS = 4
time_step = 0.2
viscosity = 0.25
MESH = pl.DeviceIdType.MESH
F32 = jnp.float32
BF16 = jnp.bfloat16

DIRS = [(dx, dy) for dx in (-1, 0, 1) for dy in (-1, 0, 1) if (dx, dy) != (0, 0)]


def div(a, b):
    return lax.div(a, jnp.int32(b))


def rem(a, b):
    return lax.rem(a, jnp.int32(b))


def device_at(x, y, z, core):
    return 2 * div(z, 4) + core, rem(z, 4) * 4 + y, x


def far_first():
    return sorted(((dx, dy) for dx in range(4) for dy in range(4)), key=lambda d: -sum(min(v, 4 - v) for v in d))


def roll(value, shift, axis):
    size = value.shape[axis]
    shift = shift % size
    return value if shift == 0 else pltpu.roll(value, shift, axis)


def lanes_of(value):
    return lax.broadcasted_iota(jnp.int32, value.shape, value.ndim - 1)


def swap_blocks(blocks):
    lane = lanes_of(blocks[0])
    blocks = list(blocks)
    for bit in (3, 2, 1, 0):
        d, width = 1 << bit, 2 << bit
        upper = (lane & width) != 0
        for i in range(16):
            if i & d:
                continue
            a, b = blocks[i], blocks[i | d]
            blocks[i] = jnp.where(upper, roll(b, width, 1), a)
            blocks[i | d] = jnp.where(upper, b, roll(a, -width, 1))
    return blocks


def take_lanes(value, index):
    return jnp.take_along_axis(value, index, axis=1, mode="promise_in_bounds")


def to_planes(blocks):
    lane = lanes_of(blocks[0])
    rest = lane % 64
    index = (rest % 4) * 32 + (rest // 4) * 2 + lane // 64
    return [take_lanes(b, index) for b in swap_blocks(blocks)]


def from_planes(blocks):
    lane = lanes_of(blocks[0])
    index = (lane % 2) * 64 + ((lane % 32) // 2) * 4 + lane // 32
    return swap_blocks([take_lanes(b, index) for b in blocks])


def pair_swap(a, b):
    upper = lanes_of(a) >= 64
    return jnp.where(upper, roll(b, 64, 1), a), jnp.where(upper, b, roll(a, 64, 1))


def split(value):
    high = value.astype(BF16)
    return high, (value - high.astype(F32)).astype(BF16)


def dot(a, b):
    return lax.dot_general(a, b, (((1,), (0,)), ((), ())), preferred_element_type=F32)


def flow_block(ref, j, lane, rows):
    def block(c, at, first, count):
        return ref[c, first:first + count, pl.ds(pl.multiple_of(at * 128, 128), 128)]

    first, count = (0, 24) if rows is None else rows
    z = lane % CZ
    centre, ax, bx, ay, by, az, bz = [], [], [], [], [], [], []
    for c in range(3):
        cur, prv, nxt = (block(c, at, first, count) for at in (j, j - 1, j + 1))
        centre.append(cur)
        if rows is None:
            ax.append(roll(cur, -1, 0))
            bx.append(roll(cur, 1, 0))
        else:
            ax.append(block(c, j, first + 1, count))
            bx.append(block(c, j, first - 1, count))
        ay.append(roll(jnp.where(lane < 32, nxt, cur), -32, 1))
        by.append(roll(jnp.where(lane < 96, cur, prv), 32, 1))
        az.append(jnp.where(z != CZ - 1, roll(cur, -1, 1), roll(cur, 31, 1)))
        bz.append(jnp.where(z != 0, roll(cur, 1, 1), roll(cur, -31, 1)))
    omega_x = 0.5 * ((ay[2] - by[2]) - (az[1] - bz[1]))
    omega_y = 0.5 * ((az[0] - bz[0]) - (ax[2] - bx[2]))
    omega_z = 0.5 * ((ax[1] - bx[1]) - (ay[0] - by[0]))
    u, v, w = centre
    lamb = [omega_y * w - omega_z * v, omega_z * u - omega_x * w, omega_x * v - omega_y * u]
    updated = []
    for c in range(3):
        laplace = ax[c] + bx[c] + ay[c] + by[c] + az[c] + bz[c] - 6.0 * centre[c]
        updated.append(centre[c] + time_step * (viscosity * laplace - lamb[c]))
    return updated, lamb


def kernel(
    coup, off, f, xo, yo, xcls, ycls, out,
    U, V, M, hxs, hxr, hyr, cs, cr, PB, A, L, X, Y, CY, CX, CYL, CXL, R, D, Q,
    XH, XL, YH, YL, SX, SY, TH, TL, AH, AL, BH, BL,
    hss, hrs, pss, ars, lrs, xss, yss, css, dss, xrs, xrs2, yrs, crs, crs2, drs, rss, rrs, known_x, known_y,
):
    sec, gx, gy = lax.axis_index("sec"), lax.axis_index("gx"), lax.axis_index("gy")
    x, y, z, core = gy, rem(gx, 4), 4 * div(sec, 2) + div(gx, 4), rem(sec, 2)
    is_flow = sec < 3
    is_owner = (core == 1) & (z != 4) & (z != 7)
    my_q = 4 * x + y
    my_m = z - (z > 4).astype(jnp.int32)
    my_o = my_m * 16 + my_q

    def remote(src, dst, ss, rs, device):
        return pltpu.make_async_remote_copy(
            src_ref=src, dst_ref=dst, send_sem=ss, recv_sem=rs, device_id=device, device_id_type=MESH
        )

    def wait_for(ref, sem):
        pltpu.make_async_copy(ref, ref, sem).wait()

    def signal(sem, device):
        pl.semaphore_signal(sem, inc=1, device_id=device, device_id_type=MESH)

    barrier = pltpu.get_barrier_semaphore()
    greeted = 0
    for dx, dy in DIRS:
        signal(barrier, (sec, rem(gx + dx + 16, 16), rem(gy + dy + 4, 4)))
        greeted += 1
    signal(barrier, device_at(rem(x + 2, 4), y, z, core))
    for d in (1, 2, 3):
        signal(barrier, device_at(x, rem(y + d, 4), z, core))
    signal(barrier, device_at(x, y, z, 1 - core))
    for d in range(1, 8):
        for c in range(2):
            signal(barrier, device_at(x, y, rem(z + d, 8), c))
    greeted += 1 + 3 + 1 + 14

    def inside(dx, dy):
        return (gx + dx >= 0) & (gx + dx < 16) & (gy + dy >= 0) & (gy + dy < 4)

    @pl.when(is_flow)
    def _():
        for c in range(3):
            for side, rows in ((0, 14), (1, 0)):
                for part in range(4):
                    hxs[side, c, 2 * part:2 * part + 2, :] = f[c, rows:rows + 2, 512 * part:512 * part + 512]
        for n, (dx, dy) in enumerate(DIRS):
            if dx and dy:
                rows, lanes = (14 if dx > 0 else 0), (1920 if dy > 0 else 0)
                for c in range(3):
                    cs[n, 2 * c:2 * c + 2, :] = f[c, rows:rows + 2, lanes:lanes + 128]
        U[...] = jnp.zeros_like(U)
        for c in range(3):
            for g in range(16):
                U[c, 2:18, 256 + 128 * g:384 + 128 * g] = f[c, :, 128 * g:128 * g + 128]
        for c in range(3):
            for j in (0, 1, 18, 19):
                V[c, :, 128 * j:128 * j + 128] = jnp.zeros((32, 128), F32)

    @pl.when(core == 1)
    def _():
        CXL[...] = jnp.zeros_like(CXL)
        CXL[:, 0:64] = jnp.broadcast_to(xcls[...].astype(F32), (8, 64))
        spread = jnp.broadcast_to(ycls[...].astype(F32), (16, 16))
        diagonal = lax.broadcasted_iota(jnp.int32, (16, 16), 0) == lax.broadcasted_iota(jnp.int32, (16, 16), 1)
        column = jnp.sum(jnp.where(diagonal, spread, 0.0), axis=1, keepdims=True)
        CYL[...] = jnp.broadcast_to(column, (16, 128))

    pl.semaphore_wait(barrier, greeted)

    def halo_copy(n):
        dx, dy = DIRS[n]
        back = DIRS.index((-dx, -dy))
        device = (sec, gx + dx, gy + dy)
        if dy == 0:
            side = 0 if dx > 0 else 1
            return remote(hxs.at[side], hxr.at[side], hss.at[n], hrs.at[back], device)
        if dx == 0:
            side = 0 if dy > 0 else 1
            lanes = pl.ds(1920, 128) if dy > 0 else pl.ds(0, 128)
            return remote(f.at[:, :, lanes], hyr.at[side], hss.at[n], hrs.at[back], device)
        return remote(cs.at[n], cr.at[back], hss.at[n], hrs.at[back], device)

    @pl.when(is_flow)
    def _():
        for n, (dx, dy) in enumerate(DIRS):
            @pl.when(inside(dx, dy))
            def _():
                halo_copy(n).start()

    lanes128 = pl.ds(gy * 128, 128)
    my_zl = div(gx, 4)

    def start(wanted, src, dst, ss, rs, device):
        @pl.when(wanted)
        def _():
            remote(src, dst, ss, rs, device).start()

    def start_here(wanted, src, dst, rs):
        @pl.when(wanted)
        def _():
            pltpu.make_async_copy(src, dst, rs).start()

    def drain(wanted, src, dst, ss, rs, device):
        @pl.when(wanted)
        def _():
            remote(src, dst, ss, rs, device).wait_send()

    def x_column(act):
        for n, dz in enumerate((-1, 1, 2, -2)):
            oz = rem(z + dz + 8, 8)
            k = div(oz - (oz > 4).astype(jnp.int32), 2)
            wanted = (core == 1) & (oz != 4) & (oz != 7)
            if n >= 2:
                wanted = wanted & (rem(x + y, 2) == n - 2)
            act(wanted, xo.at[:, k], X.at[:, my_zl, y], xss.at[n], xrs, device_at(x, y, oz, 1))
            act(wanted, CYL, CY.at[my_zl, y], css.at[n], crs, device_at(x, y, oz, 1))

    def x_along(act):
        for d in (1, 2, 3):
            device = device_at(x, rem(y + d, 4), z, 1)
            act(is_owner, X.at[:, :, y], X.at[:, :, y], xss.at[3 + d], xrs2, device)
            act(is_owner, CY.at[:, y], CY.at[:, y], css.at[3 + d], crs2, device)

    def y_along(act):
        mine_y = pl.ds(gy * 64, 64)
        for d in (1, 2, 3):
            device = device_at(rem(x + d, 4), y, z, 1)
            act(is_owner, yo.at[:, div(my_m, 2)], Y.at[:, mine_y], yss.at[d - 1], yrs, device)
            act(is_owner, CXL, CX.at[:, lanes128], dss.at[d - 1], drs, device)

    x_column(start)
    y_along(start)
    start_here(is_owner, xo.at[:, div(my_m, 2)], X.at[:, my_zl, y], xrs)
    start_here(is_owner, CYL, CY.at[my_zl, y], crs)
    start_here(is_owner, yo.at[:, div(my_m, 2)], Y.at[:, pl.ds(gy * 64, 64)], yrs)
    start_here(is_owner, CXL, CX.at[:, lanes128], drs)

    def forward_x():
        @pl.when(is_owner)
        def _():
            wait_for(X.at[:, :, y], xrs)
            wait_for(CY.at[:, y], crs)

        x_along(start)

    for d in (1, 2, 3):
        signal(known_x, device_at(rem(x + d, 4), y, z, core))

    rows8 = pl.ds(gx * 8, 8)

    def send_pieces(t, target, recv):
        layers = []
        for i in range(6):
            m = rem(z + 3 + i, 6)
            oz = m + (m >= 4).astype(jnp.int32)
            layers.append((m * 16, 2 * div(oz, 4) + 1, rem(oz, 4) * 4, m))
        for dx, dy in far_first():
            tx, ty = rem(x + dx, 4), rem(y + dy, 4)
            q = 4 * tx + ty
            for base, osec, ogx, m in layers:
                copy = remote(PB.at[t, base + q], target, pss.at[t], recv, (osec, ogx + ty, tx))
                if dx or dy:
                    copy.start()
                    continue
                mine = is_owner & (m == my_m)

                @pl.when(jnp.logical_not(mine))
                def _():
                    copy.start()

                @pl.when(mine)
                def _():
                    pltpu.make_async_copy(PB.at[t, base + q], target, recv).start()

    def drain_pieces(t):
        @pl.when(is_owner)
        def _():
            wait_for(PB.at[t, pl.ds(0, 95)], pss.at[t])

        @pl.when(jnp.logical_not(is_owner))
        def _():
            wait_for(PB.at[t], pss.at[t])

    def planes_of(src, t):
        def body(k, carry):
            blocks = to_planes([src[k, :, 128 * g:128 * g + 128] for g in range(16)])
            for q in range(16):
                even, odd = pair_swap(blocks[q][0:8], blocks[q][8:16])
                PB[t, 32 * k + q] = even
                PB[t, 32 * k + 16 + q] = odd
            return carry

        lax.fori_loop(0, 3, body, 0)

    @pl.when(sec == 3)
    def _():
        planes_of(f, 0)

    pl.semaphore_wait(known_x, 3)
    for d in (1, 2, 3):
        signal(known_y, device_at(x, rem(y + d, 4), z, core))

    lane = lax.broadcasted_iota(jnp.int32, (24, 128), 1)
    row = lax.broadcasted_iota(jnp.int32, (24, 128), 0)

    def mixed(lamb, k):
        at = jnp.minimum(sec, 2)
        total = coup[at, k, 0] * lamb[0] + coup[at, k, 1] * lamb[1] + coup[at, k, 2] * lamb[2]
        return time_step * total

    @pl.when(is_flow)
    def _():
        for n, (dx, dy) in enumerate(DIRS):
            rows = {-1: 0, 0: 2, 1: 18}[dx]
            lanes = {-1: 128, 0: 256, 1: 2304}[dy]

            @pl.when(inside(dx, dy))
            def _():
                if dy == 0:
                    side = 0 if dx < 0 else 1
                    wait_for(hxr.at[side], hrs.at[n])
                    for c in range(3):
                        for part in range(4):
                            U[c, rows:rows + 2, lanes + 512 * part:lanes + 512 * part + 512] = hxr[side, c, 2 * part:2 * part + 2, :]
                elif dx == 0:
                    side = 0 if dy < 0 else 1
                    wait_for(hyr.at[side], hrs.at[n])
                    for c in range(3):
                        U[c, 2:18, lanes:lanes + 128] = hyr[side, c]
                else:
                    wait_for(cr.at[n], hrs.at[n])
                    for c in range(3):
                        U[c, rows:rows + 2, lanes:lanes + 128] = cr[n, 2 * c:2 * c + 2, :]

    @pl.when(sec == 3)
    def _():
        pl.semaphore_wait(known_y, 3)
        send_pieces(0, A.at[rows8, lanes128], ars)
        forward_x()

    @pl.when(is_flow)
    def _():
        valid = ((row >= 2) | (gx > 0)) & ((row < 18) | (gx < 15))

        def keep(j, updated):
            at = pl.ds(pl.multiple_of(j * 128, 128), 128)
            for c in range(3):
                rolled = roll(updated[c], -2, 0)
                V[c, 8:24, at] = rolled[0:16]
                V[c, 0:8, at] = rolled[16:24]
                V[c, 24:32, at] = rolled[16:24]

        def edge(j, there):
            updated, _ = flow_block(U, j, lane, None)
            keep(j, [jnp.where(valid & there, value, 0.0) for value in updated])

        def first(j, carry):
            updated, lamb = flow_block(U, j, lane, None)
            keep(j, [jnp.where(valid, value, 0.0) for value in updated])
            for c in range(3):
                M[c, :, pl.ds(pl.multiple_of((j - 2) * 128, 128), 128)] = roll(mixed(lamb, c), -2, 0)[0:16]
            return carry

        lax.fori_loop(2, 18, first, 0, unroll=2)
        planes_of(M, 0)
        pl.semaphore_wait(known_y, 3)
        send_pieces(0, L.at[0, sec, rows8, lanes128], lrs.at[0])

        @pl.when(core == 1)
        def _():
            forward_x()

        edge(1, gy > 0)
        edge(18, gy < 3)

        def second(j, carry):
            updated, lamb = flow_block(V, j, lane[0:16], (8, 16))
            for c in range(3):
                at = pl.ds(pl.multiple_of((j - 2) * 128, 128), 128)
                out[c, :, at] = updated[c]
                M[c, :, at] = mixed(lamb, c)
            return carry

        lax.fori_loop(2, 18, second, 0, unroll=2)
        planes_of(M, 1)
        send_pieces(1, L.at[1, sec, rows8, lanes128], lrs.at[1])

    @pl.when(is_owner)
    def _():
        i = lax.broadcasted_iota(jnp.int32, (256, 256), 0)
        j = lax.broadcasted_iota(jnp.int32, (256, 256), 1)
        for s in range(3):
            d = i - j - off[0, s]
            SX[:, 256 * s:256 * s + 256] = jnp.where((d == 0) | (d == 1), 0.5, 0.0).astype(BF16)
            d = j - i - off[1, s]
            SY[s] = jnp.where((d == 0) | (d == 1), 0.5, 0.0).astype(BF16)
        wait_for(X.at[:, :, pl.ds(0, 3)], xrs2)
        wait_for(CY.at[:, pl.ds(0, 3)], crs2)
        wait_for(Y, yrs)
        wait_for(CX, drs)
        for c in range(NCLASS):
            high, low = split(X[c].reshape(256, 256))
            XH[:, 256 * c:256 * c + 256] = high
            XL[:, 256 * c:256 * c + 256] = low
            high, low = split(Y[c].T)
            YH[256 * c:256 * c + 256, :] = high
            YL[256 * c:256 * c + 256, :] = low

        def unpacked(ref):
            halves = []
            for h in range(2):
                a, b = pair_swap(ref[:, 256 * h:256 * h + 128], ref[:, 256 * h + 128:256 * h + 256])
                rows = jnp.stack([a.reshape(16, 8, 128), b.reshape(16, 8, 128)], axis=1)
                halves.append(rows.reshape(256, 128))
            return jnp.concatenate(halves, axis=1)

        column_class = jnp.concatenate(
            [pair_swap(CX[:, 256 * h:256 * h + 128], CX[:, 256 * h + 128:256 * h + 256])[0][0:1] for h in range(2)], axis=1
        )
        row_class = CY[...].reshape(256, 128)[:, 0:1]

        def add_source(t):
            for s in range(3):
                high, low = split(unpacked(L.at[t, s]))
                high, low = split(dot(high, SY[s]) + dot(low, SY[s]))
                TH[256 * s:256 * s + 256, :] = high
                TL[256 * s:256 * s + 256, :] = low
            return D[...] + dot(SX[...], TH[...]) + dot(SX[...], TL[...])

        def sweeps(value):
            high, low = split(value)
            for c in range(NCLASS):
                keep = column_class == c
                AH[256 * c:256 * c + 256, :] = jnp.where(keep, high, jnp.zeros_like(high))
                AL[256 * c:256 * c + 256, :] = jnp.where(keep, low, jnp.zeros_like(low))
            swept = dot(XH[...], AH[...]) + dot(XL[...], AH[...]) + dot(XH[...], AL[...])
            high, low = split(swept)
            for c in range(NCLASS):
                keep = row_class == c
                BH[:, 256 * c:256 * c + 256] = jnp.where(keep, high, jnp.zeros_like(high))
                BL[:, 256 * c:256 * c + 256] = jnp.where(keep, low, jnp.zeros_like(low))
            return dot(BH[...], YH[...]) + dot(BL[...], YH[...]) + dot(BH[...], YL[...])

        wait_for(A, ars)
        D[...] = unpacked(A)
        wait_for(L.at[0], lrs.at[0])
        D[...] = sweeps(add_source(0))
        wait_for(L.at[1], lrs.at[1])
        result = sweeps(add_source(1))
        for h in range(2):
            rows = result[:, 128 * h:128 * h + 128].reshape(16, 2, 8, 128)
            a, b = pair_swap(rows[:, 0].reshape(128, 128), rows[:, 1].reshape(128, 128))
            R[:, 256 * h:256 * h + 128] = a
            R[:, 256 * h + 128:256 * h + 256] = b

        for dx, dy in far_first():
            tx, ty = rem(x + dx, 4), rem(y + dy, 4)
            for i in range(4):
                zl = rem(z + 2 + i, 4)
                rows = pl.ds(pl.multiple_of((4 * zl + ty) * 8, 8), 8)
                src = R.at[rows, pl.ds(pl.multiple_of(tx * 128, 128), 128)]
                copy = remote(src, Q.at[my_o], rss, rrs, (3, 4 * zl + ty, tx))
                if dx or dy:
                    copy.start()
                    continue
                mine = (sec == 3) & (zl == my_zl)

                @pl.when(jnp.logical_not(mine))
                def _():
                    copy.start()

                @pl.when(mine)
                def _():
                    pltpu.make_async_copy(src, Q.at[my_o], rrs).start()

    @pl.when(sec == 3)
    def _():
        wait_for(Q, rrs)

        def body(k, carry):
            blocks = []
            for q in range(16):
                a, b = pair_swap(Q[32 * k + q], Q[32 * k + 16 + q])
                blocks.append(jnp.concatenate([a, b], axis=0))
            blocks = from_planes(blocks)
            for g in range(16):
                out[k, :, 128 * g:128 * g + 128] = blocks[g]
            return carry

        lax.fori_loop(0, 3, body, 0)
        drain_pieces(0)

    @pl.when(is_owner & (sec == 3))
    def _():
        wait_for(Q.at[pl.ds(0, 63)], rss)

    @pl.when(is_owner & (sec != 3))
    def _():
        wait_for(Q.at[pl.ds(0, 64)], rss)

    x_column(drain)
    x_along(drain)
    y_along(drain)

    @pl.when(is_flow)
    def _():
        for n, (dx, dy) in enumerate(DIRS):
            @pl.when(inside(dx, dy))
            def _():
                halo_copy(n).wait_send()
        for t in range(2):
            drain_pieces(t)


def local(fields, x_ops, y_ops, x_line_class, y_line_class, box_offset, coupling):
    vmem, smem, any_space = (pl.BlockSpec(memory_space=m) for m in (pltpu.VMEM, pltpu.SMEM, pl.ANY))
    V, D = pltpu.VMEM, pltpu.SemaphoreType.DMA
    out = pl.pallas_call(
        kernel,
        out_shape=jax.ShapeDtypeStruct((3, 16, 2048), F32),
        in_specs=[smem, smem, vmem, any_space, any_space, vmem, vmem],
        out_specs=vmem,
        scratch_shapes=[
            V((3, 24, 2560), F32), V((3, 32, 2560), F32), V((3, 16, 2048), F32),
            V((2, 3, 8, 512), F32), V((2, 3, 8, 512), F32), V((2, 3, 16, 128), F32),
            V((8, 8, 128), F32), V((8, 8, 128), F32),
            V((2, 96, 8, 128), F32), V((128, 512), F32), V((2, 3, 128, 512), F32),
            V((4, 4, 4, 16, 256), F32), V((4, 256, 256), F32), V((4, 4, 16, 128), F32), V((8, 512), F32),
            V((16, 128), F32), V((8, 128), F32),
            V((128, 512), F32), V((256, 256), F32), V((96, 8, 128), F32),
            V((256, 1024), BF16), V((256, 1024), BF16), V((1024, 256), BF16), V((1024, 256), BF16),
            V((256, 768), BF16), V((3, 256, 256), BF16), V((768, 256), BF16), V((768, 256), BF16),
            V((1024, 256), BF16), V((1024, 256), BF16), V((256, 1024), BF16), V((256, 1024), BF16),
            D((8,)), D((8,)), D((2,)), D, D((2,)),
            D((7,)), D((3,)), D((7,)), D((3,)), D, D, D, D, D, D, D, D,
            pltpu.SemaphoreType.REGULAR, pltpu.SemaphoreType.REGULAR,
        ],
        compiler_params=pltpu.CompilerParams(
            collective_id=0, has_side_effects=True, vmem_limit_bytes=60 << 20
        ),
    )(coupling, box_offset.T, fields[0], x_ops, y_ops, x_line_class[None], y_line_class[None])
    return out[None]


def solution(mesh):
    placed = (
        P("sec", None, "gx", "gy"),
        P(None, None, "gx", None),
        P(None, None, "gy", None),
        P("gy"),
        P("gx"),
        P(),
        P(),
    )
    return jax.shard_map(
        local, mesh=mesh, in_specs=placed, out_specs=P("sec", None, "gx", "gy"), check_vma=False
    )
```

```python
import functools

import jax
import jax.numpy as jnp
from jax import lax
from jax.experimental import pallas as pl
from jax.experimental.pallas import tpu as pltpu
from jax.sharding import PartitionSpec as P

CZ = 32
NCLASS = 4
time_step = 0.2
viscosity = 0.25
MESH = pl.DeviceIdType.MESH
F32 = jnp.float32
BF16 = jnp.bfloat16

DIRS = [(dx, dy) for dx in (-1, 0, 1) for dy in (-1, 0, 1) if (dx, dy) != (0, 0)]


def div(a, b):
    return lax.div(a, jnp.int32(b))


def rem(a, b):
    return lax.rem(a, jnp.int32(b))


def device_at(x, y, z, core):
    return 2 * div(z, 4) + core, rem(z, 4) * 4 + y, x


def far_first():
    return sorted(((dx, dy) for dx in range(4) for dy in range(4)), key=lambda d: -sum(min(v, 4 - v) for v in d))


def roll(value, shift, axis):
    size = value.shape[axis]
    shift = shift % size
    return value if shift == 0 else pltpu.roll(value, shift, axis)


def lanes_of(value):
    return lax.broadcasted_iota(jnp.int32, value.shape, value.ndim - 1)


def swap_blocks(blocks):
    lane = lanes_of(blocks[0])
    blocks = list(blocks)
    for bit in (3, 2, 1, 0):
        d, width = 1 << bit, 2 << bit
        upper = (lane & width) != 0
        for i in range(16):
            if i & d:
                continue
            a, b = blocks[i], blocks[i | d]
            crossing = take_lanes(jnp.where(upper, a, b), lane ^ width)
            blocks[i] = jnp.where(upper, crossing, a)
            blocks[i | d] = jnp.where(upper, b, crossing)
    return blocks


def take_lanes(value, index):
    return jnp.take_along_axis(value, index, axis=1, mode="promise_in_bounds")


def to_planes(blocks):
    lane = lanes_of(blocks[0])
    rest = lane % 64
    index = (rest % 4) * 32 + (rest // 4) * 2 + lane // 64
    return [take_lanes(b, index) for b in swap_blocks(blocks)]


def from_planes(blocks):
    lane = lanes_of(blocks[0])
    index = (lane % 2) * 64 + ((lane % 32) // 2) * 4 + lane // 32
    return swap_blocks([take_lanes(b, index) for b in blocks])


def pair_swap(a, b):
    upper = lanes_of(a) >= 64
    crossing = roll(jnp.where(upper, a, b), 64, 1)
    return jnp.where(upper, crossing, a), jnp.where(upper, b, crossing)


def split(value):
    high = value.astype(BF16)
    return high, (value - high.astype(F32)).astype(BF16)


def dot(a, b):
    return lax.dot_general(a, b, (((1,), (0,)), ((), ())), preferred_element_type=F32)


def flow_block(ref, j, lane, rows):
    def block(c, at, first, count):
        return ref[c, first:first + count, pl.ds(pl.multiple_of(at * 128, 128), 128)]

    first, count = (0, 24) if rows is None else rows
    z = lane % CZ
    centre, ax, bx, ay, by, az, bz = [], [], [], [], [], [], []
    for c in range(3):
        cur, prv, nxt = (block(c, at, first, count) for at in (j, j - 1, j + 1))
        centre.append(cur)
        if rows is None:
            ax.append(roll(cur, -1, 0))
            bx.append(roll(cur, 1, 0))
        else:
            ax.append(block(c, j, first + 1, count))
            bx.append(block(c, j, first - 1, count))
        ay.append(roll(jnp.where(lane < 32, nxt, cur), -32, 1))
        by.append(roll(jnp.where(lane < 96, cur, prv), 32, 1))
        az.append(jnp.where(z != CZ - 1, roll(cur, -1, 1), roll(cur, 31, 1)))
        bz.append(jnp.where(z != 0, roll(cur, 1, 1), roll(cur, -31, 1)))
    omega_x = 0.5 * ((ay[2] - by[2]) - (az[1] - bz[1]))
    omega_y = 0.5 * ((az[0] - bz[0]) - (ax[2] - bx[2]))
    omega_z = 0.5 * ((ax[1] - bx[1]) - (ay[0] - by[0]))
    u, v, w = centre
    lamb = [omega_y * w - omega_z * v, omega_z * u - omega_x * w, omega_x * v - omega_y * u]
    updated = []
    for c in range(3):
        laplace = ax[c] + bx[c] + ay[c] + by[c] + az[c] + bz[c] - 6.0 * centre[c]
        updated.append(centre[c] + time_step * (viscosity * laplace - lamb[c]))
    return updated, lamb


def kernel(
    coup, off, f, xo, yo, xcls, ycls, out,
    U, V, M, hxs, hxr, hyr, cs, cr, PB, A, L, X, Y, CY, CX, CYL, CXL, R, D, Q,
    XH, XL, YH, YL, SX, SY, TH, TL, AH, AL, BH, BL,
    hss, hrs, pss, ars, lrs, xss, yss, css, dss, xrs, xrs2, yrs, crs, crs2, drs, rss, rrs, known_z, known_x, known_y,
):
    sec, gx, gy = lax.axis_index("sec"), lax.axis_index("gx"), lax.axis_index("gy")
    x, y, z, core = gy, rem(gx, 4), 4 * div(sec, 2) + div(gx, 4), rem(sec, 2)
    is_flow = sec < 3
    is_owner = (core == 1) & (z != 4) & (z != 7)
    my_q = 4 * x + y
    my_m = z - (z > 4).astype(jnp.int32)
    my_o = my_m * 16 + my_q

    def remote(src, dst, ss, rs, device):
        return pltpu.make_async_remote_copy(
            src_ref=src, dst_ref=dst, send_sem=ss, recv_sem=rs, device_id=device, device_id_type=MESH
        )

    def wait_for(ref, sem):
        pltpu.make_async_copy(ref, ref, sem).wait()

    def signal(sem, device):
        pl.semaphore_signal(sem, inc=1, device_id=device, device_id_type=MESH)

    barrier = pltpu.get_barrier_semaphore()

    def inside(dx, dy):
        return (gx + dx >= 0) & (gx + dx < 16) & (gy + dy >= 0) & (gy + dy < 4)

    greeted = 0
    for dx, dy in DIRS:
        @pl.when(inside(dx, dy))
        def _():
            signal(barrier, (sec, gx + dx, gy + dy))
        greeted += inside(dx, dy).astype(jnp.int32)
    for d in (1, 2, 3):
        signal(barrier, device_at(rem(x + d, 4), y, z, core))
        signal(barrier, device_at(x, rem(y + d, 4), z, core))
    signal(barrier, device_at(x, y, z, 1 - core))
    for d in (-2, -1, 1, 2):
        for c in range(2):
            signal(barrier, device_at(x, y, rem(z + d + 8, 8), c))
    greeted += 6 + 1 + 8

    @pl.when(is_flow)
    def _():
        for c in range(3):
            for side, rows in ((0, 14), (1, 0)):
                for part in range(4):
                    hxs[side, c, 2 * part:2 * part + 2, :] = f[c, rows:rows + 2, 512 * part:512 * part + 512]
        for n, (dx, dy) in enumerate(DIRS):
            if dx and dy:
                rows, lanes = (14 if dx > 0 else 0), (1920 if dy > 0 else 0)
                for c in range(3):
                    cs[n, 2 * c:2 * c + 2, :] = f[c, rows:rows + 2, lanes:lanes + 128]
        U[...] = jnp.zeros_like(U)
        for c in range(3):
            for g in range(16):
                U[c, 2:18, 256 + 128 * g:384 + 128 * g] = f[c, :, 128 * g:128 * g + 128]
        for c in range(3):
            for j in (0, 1, 18, 19):
                V[c, :, 128 * j:128 * j + 128] = jnp.zeros((32, 128), F32)

    @pl.when(core == 1)
    def _():
        CXL[...] = jnp.zeros_like(CXL)
        CXL[:, 0:64] = jnp.broadcast_to(xcls[...].astype(F32), (8, 64))
        spread = jnp.broadcast_to(ycls[...].astype(F32), (16, 16))
        diagonal = lax.broadcasted_iota(jnp.int32, (16, 16), 0) == lax.broadcasted_iota(jnp.int32, (16, 16), 1)
        column = jnp.sum(jnp.where(diagonal, spread, 0.0), axis=1, keepdims=True)
        CYL[...] = jnp.broadcast_to(column, (16, 128))

    pl.semaphore_wait(barrier, greeted)

    def halo_copy(n):
        dx, dy = DIRS[n]
        back = DIRS.index((-dx, -dy))
        device = (sec, gx + dx, gy + dy)
        if dy == 0:
            side = 0 if dx > 0 else 1
            return remote(hxs.at[side], hxr.at[side], hss.at[n], hrs.at[back], device)
        if dx == 0:
            side = 0 if dy > 0 else 1
            lanes = pl.ds(1920, 128) if dy > 0 else pl.ds(0, 128)
            return remote(f.at[:, :, lanes], hyr.at[side], hss.at[n], hrs.at[back], device)
        return remote(cs.at[n], cr.at[back], hss.at[n], hrs.at[back], device)

    @pl.when(is_flow)
    def _():
        for n, (dx, dy) in enumerate(DIRS):
            @pl.when(inside(dx, dy))
            def _():
                halo_copy(n).start()

    lanes128 = pl.ds(gy * 128, 128)
    my_zl = div(gx, 4)

    def start(wanted, src, dst, ss, rs, device):
        @pl.when(wanted)
        def _():
            remote(src, dst, ss, rs, device).start()

    def start_here(wanted, src, dst, rs):
        @pl.when(wanted)
        def _():
            pltpu.make_async_copy(src, dst, rs).start()

    def drain(wanted, src, dst, ss, rs, device):
        @pl.when(wanted)
        def _():
            remote(src, dst, ss, rs, device).wait_send()

    def x_column(act):
        for n, dz in enumerate((-1, 1, 2, -2)):
            oz = rem(z + dz + 8, 8)
            k = div(oz - (oz > 4).astype(jnp.int32), 2)
            wanted = (core == 1) & (oz != 4) & (oz != 7)
            if n >= 2:
                wanted = wanted & (rem(x + y, 2) == n - 2)
            act(wanted, xo.at[:, k], X.at[:, my_zl, y], xss.at[n], xrs, device_at(x, y, oz, 1))
            act(wanted, CYL, CY.at[my_zl, y], css.at[n], crs, device_at(x, y, oz, 1))

    def x_along(act):
        for d in (1, 2, 3):
            device = device_at(x, rem(y + d, 4), z, 1)
            act(is_owner, X.at[:, :, y], X.at[:, :, y], xss.at[3 + d], xrs2, device)
            act(is_owner, CY.at[:, y], CY.at[:, y], css.at[3 + d], crs2, device)

    def y_along(act):
        mine_y = pl.ds(gy * 64, 64)
        for d in (1, 2, 3):
            device = device_at(rem(x + d, 4), y, z, 1)
            act(is_owner, yo.at[:, div(my_m, 2)], Y.at[:, mine_y], yss.at[d - 1], yrs, device)
            act(is_owner, CXL, CX.at[:, lanes128], dss.at[d - 1], drs, device)

    x_column(start)
    y_along(start)
    start_here(is_owner, xo.at[:, div(my_m, 2)], X.at[:, my_zl, y], xrs)
    start_here(is_owner, CYL, CY.at[my_zl, y], crs)
    start_here(is_owner, yo.at[:, div(my_m, 2)], Y.at[:, pl.ds(gy * 64, 64)], yrs)
    start_here(is_owner, CXL, CX.at[:, lanes128], drs)

    def forward_x():
        @pl.when(is_owner)
        def _():
            wait_for(X.at[:, :, y], xrs)
            wait_for(CY.at[:, y], crs)

        x_along(start)

    for d in (-2, -1, 1, 2):
        signal(known_z, device_at(x, y, rem(z + d + 8, 8), core))

    rows8 = pl.ds(gx * 8, 8)

    def send_planes(src, t, target, recv, ready):
        first_k = rem(div(z, 2) + 1, 3)
        for i in range(3):
            k = rem(first_k + i, 3)
            blocks = to_planes([src[k, :, 128 * g:128 * g + 128] for g in range(16)])
            for q in range(16):
                even, odd = pair_swap(blocks[q][0:8], blocks[q][8:16])
                PB[t, 32 * k + q] = even
                PB[t, 32 * k + 16 + q] = odd
            if i == 0:
                ready()
            layers = []
            for parity in range(2):
                m = 2 * k + parity
                oz = m + (m >= 4).astype(jnp.int32)
                layers.append((m * 16, 2 * div(oz, 4) + 1, rem(oz, 4) * 4, m))
            for dx, dy in far_first():
                tx, ty = rem(x + dx, 4), rem(y + dy, 4)
                q = 4 * tx + ty
                for base, osec, ogx, m in layers:
                    copy = remote(PB.at[t, base + q], target, pss.at[t], recv, (osec, ogx + ty, tx))
                    if dx or dy:
                        copy.start()
                        continue
                    mine = is_owner & (m == my_m)

                    @pl.when(jnp.logical_not(mine))
                    def _():
                        copy.start()

                    @pl.when(mine)
                    def _():
                        pltpu.make_async_copy(PB.at[t, base + q], target, recv).start()

    def everyone():
        pl.semaphore_wait(known_y, 3)

    def drain_pieces(t):
        @pl.when(is_owner)
        def _():
            wait_for(PB.at[t, pl.ds(0, 95)], pss.at[t])

        @pl.when(jnp.logical_not(is_owner))
        def _():
            wait_for(PB.at[t], pss.at[t])

    pl.semaphore_wait(known_z, 4)
    for d in (1, 2, 3):
        signal(known_x, device_at(rem(x + d, 4), y, z, core))

    lane = lax.broadcasted_iota(jnp.int32, (24, 128), 1)
    row = lax.broadcasted_iota(jnp.int32, (24, 128), 0)

    def mixed(lamb, k):
        at = jnp.minimum(sec, 2)
        total = coup[at, k, 0] * lamb[0] + coup[at, k, 1] * lamb[1] + coup[at, k, 2] * lamb[2]
        return time_step * total

    @pl.when(is_flow)
    def _():
        for n, (dx, dy) in enumerate(DIRS):
            rows = {-1: 0, 0: 2, 1: 18}[dx]
            lanes = {-1: 128, 0: 256, 1: 2304}[dy]

            @pl.when(inside(dx, dy))
            def _():
                if dy == 0:
                    side = 0 if dx < 0 else 1
                    wait_for(hxr.at[side], hrs.at[n])
                    for c in range(3):
                        for part in range(4):
                            U[c, rows:rows + 2, lanes + 512 * part:lanes + 512 * part + 512] = hxr[side, c, 2 * part:2 * part + 2, :]
                elif dx == 0:
                    side = 0 if dy < 0 else 1
                    wait_for(hyr.at[side], hrs.at[n])
                    for c in range(3):
                        U[c, 2:18, lanes:lanes + 128] = hyr[side, c]
                else:
                    wait_for(cr.at[n], hrs.at[n])
                    for c in range(3):
                        U[c, rows:rows + 2, lanes:lanes + 128] = cr[n, 2 * c:2 * c + 2, :]

    pl.semaphore_wait(known_x, 3)
    for d in (1, 2, 3):
        signal(known_y, device_at(x, rem(y + d, 4), z, core))

    @pl.when(sec == 3)
    def _():
        send_planes(f, 0, A.at[rows8, lanes128], ars, everyone)
        forward_x()

    @pl.when(is_flow)
    def _():
        valid = ((row >= 2) | (gx > 0)) & ((row < 18) | (gx < 15))

        def keep(j, updated):
            at = pl.ds(pl.multiple_of(j * 128, 128), 128)
            for c in range(3):
                rolled = roll(updated[c], -2, 0)
                V[c, 8:24, at] = rolled[0:16]
                V[c, 0:8, at] = rolled[16:24]
                V[c, 24:32, at] = rolled[16:24]

        def edge(j, there):
            updated, _ = flow_block(U, j, lane, None)
            keep(j, [jnp.where(valid & there, value, 0.0) for value in updated])

        def first(j, carry):
            updated, lamb = flow_block(U, j, lane, None)
            keep(j, [jnp.where(valid, value, 0.0) for value in updated])
            for c in range(3):
                M[c, :, pl.ds(pl.multiple_of((j - 2) * 128, 128), 128)] = roll(mixed(lamb, c), -2, 0)[0:16]
            return carry

        lax.fori_loop(2, 18, first, 0, unroll=2)
        send_planes(M, 0, L.at[0, sec, rows8, lanes128], lrs.at[0], everyone)

        @pl.when(core == 1)
        def _():
            forward_x()

        edge(1, gy > 0)
        edge(18, gy < 3)

        def second(j, carry):
            updated, lamb = flow_block(V, j, lane[0:16], (8, 16))
            for c in range(3):
                at = pl.ds(pl.multiple_of((j - 2) * 128, 128), 128)
                out[c, :, at] = updated[c]
                M[c, :, at] = mixed(lamb, c)
            return carry

        lax.fori_loop(2, 18, second, 0, unroll=2)
        send_planes(M, 1, L.at[1, sec, rows8, lanes128], lrs.at[1], lambda: None)

    @pl.when(is_owner)
    def _():
        i = lax.broadcasted_iota(jnp.int32, (256, 256), 0)
        j = lax.broadcasted_iota(jnp.int32, (256, 256), 1)
        for s in range(3):
            d = i - j - off[0, s]
            SX[:, 256 * s:256 * s + 256] = jnp.where((d == 0) | (d == 1), 0.5, 0.0).astype(BF16)
            d = j - i - off[1, s]
            SY[s] = jnp.where((d == 0) | (d == 1), 0.5, 0.0).astype(BF16)
        wait_for(X.at[:, :, pl.ds(0, 3)], xrs2)
        wait_for(CY.at[:, pl.ds(0, 3)], crs2)
        wait_for(Y, yrs)
        wait_for(CX, drs)
        for c in range(NCLASS):
            high, low = split(X[c].reshape(256, 256))
            XH[:, 256 * c:256 * c + 256] = high
            XL[:, 256 * c:256 * c + 256] = low
            high, low = split(Y[c].T)
            YH[256 * c:256 * c + 256, :] = high
            YL[256 * c:256 * c + 256, :] = low

        def unpacked(ref):
            halves = []
            for h in range(2):
                a, b = pair_swap(ref[:, 256 * h:256 * h + 128], ref[:, 256 * h + 128:256 * h + 256])
                rows = jnp.stack([a.reshape(16, 8, 128), b.reshape(16, 8, 128)], axis=1)
                halves.append(rows.reshape(256, 128))
            return jnp.concatenate(halves, axis=1)

        column_class = jnp.concatenate(
            [pair_swap(CX[:, 256 * h:256 * h + 128], CX[:, 256 * h + 128:256 * h + 256])[0][0:1] for h in range(2)], axis=1
        )
        row_class = CY[...].reshape(256, 128)[:, 0:1]

        def add_source(t):
            for s in range(3):
                high, low = split(unpacked(L.at[t, s]))
                high, low = split(dot(high, SY[s]) + dot(low, SY[s]))
                TH[256 * s:256 * s + 256, :] = high
                TL[256 * s:256 * s + 256, :] = low
            return D[...] + dot(SX[...], TH[...]) + dot(SX[...], TL[...])

        def sweeps(value):
            high, low = split(value)
            for c in range(NCLASS):
                keep = column_class == c
                AH[256 * c:256 * c + 256, :] = jnp.where(keep, high, jnp.zeros_like(high))
                AL[256 * c:256 * c + 256, :] = jnp.where(keep, low, jnp.zeros_like(low))
            swept = dot(XH[...], AH[...]) + dot(XL[...], AH[...]) + dot(XH[...], AL[...])
            high, low = split(swept)
            for c in range(NCLASS):
                keep = row_class == c
                BH[:, 256 * c:256 * c + 256] = jnp.where(keep, high, jnp.zeros_like(high))
                BL[:, 256 * c:256 * c + 256] = jnp.where(keep, low, jnp.zeros_like(low))
            return dot(BH[...], YH[...]) + dot(BL[...], YH[...]) + dot(BH[...], YL[...])

        wait_for(A, ars)
        D[...] = unpacked(A)
        wait_for(L.at[0], lrs.at[0])
        D[...] = sweeps(add_source(0))
        wait_for(L.at[1], lrs.at[1])
        result = sweeps(add_source(1))
        for h in range(2):
            rows = result[:, 128 * h:128 * h + 128].reshape(16, 2, 8, 128)
            a, b = pair_swap(rows[:, 0].reshape(128, 128), rows[:, 1].reshape(128, 128))
            R[:, 256 * h:256 * h + 128] = a
            R[:, 256 * h + 128:256 * h + 256] = b

        for dx, dy in far_first():
            tx, ty = rem(x + dx, 4), rem(y + dy, 4)
            for i in range(4):
                zl = rem(z + 2 + i, 4)
                rows = pl.ds(pl.multiple_of((4 * zl + ty) * 8, 8), 8)
                src = R.at[rows, pl.ds(pl.multiple_of(tx * 128, 128), 128)]
                copy = remote(src, Q.at[my_o], rss, rrs, (3, 4 * zl + ty, tx))
                if dx or dy:
                    copy.start()
                    continue
                mine = (sec == 3) & (zl == my_zl)

                @pl.when(jnp.logical_not(mine))
                def _():
                    copy.start()

                @pl.when(mine)
                def _():
                    pltpu.make_async_copy(src, Q.at[my_o], rrs).start()

    @pl.when(sec == 3)
    def _():
        wait_for(Q, rrs)

        def body(k, carry):
            blocks = []
            for q in range(16):
                a, b = pair_swap(Q[32 * k + q], Q[32 * k + 16 + q])
                blocks.append(jnp.concatenate([a, b], axis=0))
            blocks = from_planes(blocks)
            for g in range(16):
                out[k, :, 128 * g:128 * g + 128] = blocks[g]
            return carry

        lax.fori_loop(0, 3, body, 0)
        drain_pieces(0)

    @pl.when(is_owner & (sec == 3))
    def _():
        wait_for(Q.at[pl.ds(0, 63)], rss)

    @pl.when(is_owner & (sec != 3))
    def _():
        wait_for(Q.at[pl.ds(0, 64)], rss)

    x_column(drain)
    x_along(drain)
    y_along(drain)

    @pl.when(is_flow)
    def _():
        for n, (dx, dy) in enumerate(DIRS):
            @pl.when(inside(dx, dy))
            def _():
                halo_copy(n).wait_send()
        for t in range(2):
            drain_pieces(t)


def local(fields, x_ops, y_ops, x_line_class, y_line_class, box_offset, coupling):
    vmem, smem, any_space = (pl.BlockSpec(memory_space=m) for m in (pltpu.VMEM, pltpu.SMEM, pl.ANY))
    V, D = pltpu.VMEM, pltpu.SemaphoreType.DMA
    out = pl.pallas_call(
        kernel,
        out_shape=jax.ShapeDtypeStruct((3, 16, 2048), F32),
        in_specs=[smem, smem, vmem, any_space, any_space, vmem, vmem],
        out_specs=vmem,
        scratch_shapes=[
            V((3, 24, 2560), F32), V((3, 32, 2560), F32), V((3, 16, 2048), F32),
            V((2, 3, 8, 512), F32), V((2, 3, 8, 512), F32), V((2, 3, 16, 128), F32),
            V((8, 8, 128), F32), V((8, 8, 128), F32),
            V((2, 96, 8, 128), F32), V((128, 512), F32), V((2, 3, 128, 512), F32),
            V((4, 4, 4, 16, 256), F32), V((4, 256, 256), F32), V((4, 4, 16, 128), F32), V((8, 512), F32),
            V((16, 128), F32), V((8, 128), F32),
            V((128, 512), F32), V((256, 256), F32), V((96, 8, 128), F32),
            V((256, 1024), BF16), V((256, 1024), BF16), V((1024, 256), BF16), V((1024, 256), BF16),
            V((256, 768), BF16), V((3, 256, 256), BF16), V((768, 256), BF16), V((768, 256), BF16),
            V((1024, 256), BF16), V((1024, 256), BF16), V((256, 1024), BF16), V((256, 1024), BF16),
            D((8,)), D((8,)), D((2,)), D, D((2,)),
            D((7,)), D((3,)), D((7,)), D((3,)), D, D, D, D, D, D, D, D,
            pltpu.SemaphoreType.REGULAR, pltpu.SemaphoreType.REGULAR, pltpu.SemaphoreType.REGULAR,
        ],
        compiler_params=pltpu.CompilerParams(
            collective_id=0, has_side_effects=True, vmem_limit_bytes=60 << 20
        ),
    )(coupling, box_offset.T, fields[0], x_ops, y_ops, x_line_class[None], y_line_class[None])
    return out[None]


def solution(mesh):
    placed = (
        P("sec", None, "gx", "gy"),
        P(None, None, "gx", None),
        P(None, None, "gy", None),
        P("gy"),
        P("gx"),
        P(),
        P(),
    )
    return jax.shard_map(
        local, mesh=mesh, in_specs=placed, out_specs=P("sec", None, "gx", "gy"), check_vma=False
    )
```

```python
import functools

import jax
import jax.numpy as jnp
from jax import lax
from jax.experimental import pallas as pl
from jax.experimental.pallas import tpu as pltpu
from jax.sharding import PartitionSpec as P

CZ = 32
NCLASS = 4
PARTS = 1
time_step = 0.2
viscosity = 0.25
MESH = pl.DeviceIdType.MESH
F32 = jnp.float32
BF16 = jnp.bfloat16

DIRS = [(dx, dy) for dx in (-1, 0, 1) for dy in (-1, 0, 1) if (dx, dy) != (0, 0)]


def div(a, b):
    return lax.div(a, jnp.int32(b))


def rem(a, b):
    return lax.rem(a, jnp.int32(b))


def device_at(x, y, z, core):
    return 2 * div(z, 4) + core, rem(z, 4) * 4 + y, x


def far_first():
    return sorted(((dx, dy) for dx in range(4) for dy in range(4)), key=lambda d: -sum(min(v, 4 - v) for v in d))


def roll(value, shift, axis):
    size = value.shape[axis]
    shift = shift % size
    return value if shift == 0 else pltpu.roll(value, shift, axis)


def lanes_of(value):
    return lax.broadcasted_iota(jnp.int32, value.shape, value.ndim - 1)


def swap_blocks(blocks):
    lane = lanes_of(blocks[0])
    blocks = list(blocks)
    for bit in (3, 2, 1, 0):
        d, width = 1 << bit, 2 << bit
        upper = (lane & width) != 0
        for i in range(16):
            if i & d:
                continue
            a, b = blocks[i], blocks[i | d]
            crossing = take_lanes(jnp.where(upper, a, b), lane ^ width)
            blocks[i] = jnp.where(upper, crossing, a)
            blocks[i | d] = jnp.where(upper, b, crossing)
    return blocks


def take_lanes(value, index):
    return jnp.take_along_axis(value, index, axis=1, mode="promise_in_bounds")


def to_planes(blocks):
    lane = lanes_of(blocks[0])
    rest = lane % 64
    index = (rest % 4) * 32 + (rest // 4) * 2 + lane // 64
    return [take_lanes(b, index) for b in swap_blocks(blocks)]


def from_planes(blocks):
    lane = lanes_of(blocks[0])
    index = (lane % 2) * 64 + ((lane % 32) // 2) * 4 + lane // 32
    return swap_blocks([take_lanes(b, index) for b in blocks])


def pair_swap(a, b):
    upper = lanes_of(a) >= 64
    crossing = roll(jnp.where(upper, a, b), 64, 1)
    return jnp.where(upper, crossing, a), jnp.where(upper, b, crossing)


def split(value):
    high = value.astype(BF16)
    return high, (value - high.astype(F32)).astype(BF16)


def dot(a, b):
    return lax.dot_general(a, b, (((1,), (0,)), ((), ())), preferred_element_type=F32)


def flow_block(ref, j, lane, rows):
    def block(c, at, first, count):
        return ref[c, first:first + count, pl.ds(pl.multiple_of(at * 128, 128), 128)]

    first, count = (0, 24) if rows is None else rows
    z = lane % CZ
    centre, ax, bx, ay, by, az, bz = [], [], [], [], [], [], []
    for c in range(3):
        cur, prv, nxt = (block(c, at, first, count) for at in (j, j - 1, j + 1))
        centre.append(cur)
        if rows is None:
            ax.append(roll(cur, -1, 0))
            bx.append(roll(cur, 1, 0))
        else:
            ax.append(block(c, j, first + 1, count))
            bx.append(block(c, j, first - 1, count))
        ay.append(roll(jnp.where(lane < 32, nxt, cur), -32, 1))
        by.append(roll(jnp.where(lane < 96, cur, prv), 32, 1))
        az.append(jnp.where(z != CZ - 1, roll(cur, -1, 1), roll(cur, 31, 1)))
        bz.append(jnp.where(z != 0, roll(cur, 1, 1), roll(cur, -31, 1)))
    omega_x = 0.5 * ((ay[2] - by[2]) - (az[1] - bz[1]))
    omega_y = 0.5 * ((az[0] - bz[0]) - (ax[2] - bx[2]))
    omega_z = 0.5 * ((ax[1] - bx[1]) - (ay[0] - by[0]))
    u, v, w = centre
    lamb = [omega_y * w - omega_z * v, omega_z * u - omega_x * w, omega_x * v - omega_y * u]
    updated = []
    for c in range(3):
        laplace = ax[c] + bx[c] + ay[c] + by[c] + az[c] + bz[c] - 6.0 * centre[c]
        updated.append(centre[c] + time_step * (viscosity * laplace - lamb[c]))
    return updated, lamb


def kernel(
    coup, off, fields, xo, yo, xcls, ycls, out,
    f, U, V, M, hxs, hxr, hyr, cs, cr, PB, A, L, X, Y, CY, CX, CYL, CXL, R, D, Q,
    XHH, XL, YHH, YL, SX, SY, TT, AA, BB,
    load, hss, hrs, pss, ars, lrs, xss, yss, css, dss, xrs, xrs2, yrs, crs, crs2, drs, rss, rrs, known_x, known_y,
):
    sec, gx, gy = lax.axis_index("sec"), lax.axis_index("gx"), lax.axis_index("gy")
    x, y, z, core = gy, rem(gx, 4), 4 * div(sec, 2) + div(gx, 4), rem(sec, 2)
    is_flow = sec < 3
    is_owner = (core == 1) & (z != 4) & (z != 7)
    is_helper = (core == 0) & (z != 4) & (z != 7)
    my_q = 4 * x + y
    my_m = z - (z > 4).astype(jnp.int32)
    my_o = my_m * 16 + my_q

    def remote(src, dst, ss, rs, device):
        return pltpu.make_async_remote_copy(
            src_ref=src, dst_ref=dst, send_sem=ss, recv_sem=rs, device_id=device, device_id_type=MESH
        )

    def wait_for(ref, sem):
        pltpu.make_async_copy(ref, ref, sem).wait()

    def signal(sem, device):
        pl.semaphore_signal(sem, inc=1, device_id=device, device_id_type=MESH)

    barrier = pltpu.get_barrier_semaphore()

    def inside(dx, dy):
        return (gx + dx >= 0) & (gx + dx < 16) & (gy + dy >= 0) & (gy + dy < 4)

    greeted = 0
    for dx, dy in DIRS:
        @pl.when(inside(dx, dy))
        def _():
            signal(barrier, (sec, gx + dx, gy + dy))
        greeted += inside(dx, dy).astype(jnp.int32)
    for d in (1, 2, 3):
        signal(barrier, device_at(rem(x + d, 4), y, z, 0))
        signal(barrier, device_at(rem(x + d, 4), y, z, 1))
        signal(barrier, device_at(x, rem(y + d, 4), z, core))
    signal(barrier, device_at(x, y, z, 1 - core))
    for d in range(1, 8):
        for c in range(2):
            signal(barrier, device_at(x, y, rem(z + d, 8), c))
    greeted += 9 + 1 + 14
    loading = pltpu.make_async_copy(fields, f, load)
    loading.start()

    CXL[...] = jnp.zeros_like(CXL)
    CXL[:, 0:64] = jnp.broadcast_to(xcls[...].astype(F32), (8, 64))
    spread = jnp.broadcast_to(ycls[...].astype(F32), (16, 16))
    diagonal = lax.broadcasted_iota(jnp.int32, (16, 16), 0) == lax.broadcasted_iota(jnp.int32, (16, 16), 1)
    column = jnp.sum(jnp.where(diagonal, spread, 0.0), axis=1, keepdims=True)
    CYL[...] = jnp.broadcast_to(column, (16, 128))

    def relay_planes(src, t, k):
        blocks = to_planes([src[k, :, 128 * g:128 * g + 128] for g in range(16)])
        for q in range(16):
            even, odd = pair_swap(blocks[q][0:8], blocks[q][8:16])
            PB[t, 32 * k + q] = even
            PB[t, 32 * k + 16 + q] = odd

    loading.wait()

    @pl.when(sec == 3)
    def _():
        lax.fori_loop(0, 3, lambda k, carry: (relay_planes(f, 0, k), carry)[1], 0)

    @pl.when(is_flow)
    def _():
        for c in range(3):
            for side, rows in ((0, 14), (1, 0)):
                for part in range(4):
                    hxs[side, c, 2 * part:2 * part + 2, :] = f[c, rows:rows + 2, 512 * part:512 * part + 512]
        for n, (dx, dy) in enumerate(DIRS):
            if dx and dy:
                rows, lanes = (14 if dx > 0 else 0), (1920 if dy > 0 else 0)
                for c in range(3):
                    cs[n, 2 * c:2 * c + 2, :] = f[c, rows:rows + 2, lanes:lanes + 128]

    pl.semaphore_wait(barrier, greeted)

    for d in (1, 2, 3):
        signal(known_x, device_at(rem(x + d, 4), y, z, core))

    def halo_copy(n):
        dx, dy = DIRS[n]
        back = DIRS.index((-dx, -dy))
        device = (sec, gx + dx, gy + dy)
        if dy == 0:
            side = 0 if dx > 0 else 1
            return remote(hxs.at[side], hxr.at[side], hss.at[n], hrs.at[back], device)
        if dx == 0:
            side = 0 if dy > 0 else 1
            lanes = pl.ds(1920, 128) if dy > 0 else pl.ds(0, 128)
            return remote(f.at[:, :, lanes], hyr.at[side], hss.at[n], hrs.at[back], device)
        return remote(cs.at[n], cr.at[back], hss.at[n], hrs.at[back], device)

    @pl.when(is_flow)
    def _():
        for n, (dx, dy) in enumerate(DIRS):
            @pl.when(inside(dx, dy))
            def _():
                halo_copy(n).start()

    lanes128 = pl.ds(gy * 128, 128)
    my_zl = div(gx, 4)

    def start(wanted, src, dst, ss, rs, device):
        @pl.when(wanted)
        def _():
            remote(src, dst, ss, rs, device).start()

    def start_here(wanted, src, dst, rs):
        @pl.when(wanted)
        def _():
            pltpu.make_async_copy(src, dst, rs).start()

    def drain(wanted, src, dst, ss, rs, device):
        @pl.when(wanted)
        def _():
            remote(src, dst, ss, rs, device).wait_send()

    def x_column(act):
        for n, dz in enumerate((-1, 1, 2, -2)):
            oz = rem(z + dz + 8, 8)
            k = div(oz - (oz > 4).astype(jnp.int32), 2)
            wanted = (core == 1) & (oz != 4) & (oz != 7)
            if n >= 2:
                wanted = wanted & (rem(x + y, 2) == n - 2)
            act(wanted, xo.at[:, k], X.at[:, my_zl, y], xss.at[n], xrs, device_at(x, y, oz, 1))
            act(wanted, CYL, CY.at[my_zl, y], css.at[n], crs, device_at(x, y, oz, 1))

    def x_along(act):
        for d in (1, 2, 3):
            device = device_at(x, rem(y + d, 4), z, 1)
            act(is_owner, X.at[:, :, y], X.at[:, :, y], xss.at[3 + d], xrs2, device)
            act(is_owner, CY.at[:, y], CY.at[:, y], css.at[3 + d], crs2, device)

    def y_along(act):
        mine_y = pl.ds(gy * 64, 64)
        for d in (1, 2, 3):
            device = device_at(rem(x + d, 4), y, z, 1)
            act(is_helper, yo.at[:, div(my_m, 2)], Y.at[:, mine_y], yss.at[d - 1], yrs, device)
            act(is_helper, CXL, CX.at[:, lanes128], dss.at[d - 1], drs, device)

    x_column(start)
    y_along(start)
    start_here(is_owner, xo.at[:, div(my_m, 2)], X.at[:, my_zl, y], xrs)
    start_here(is_owner, CYL, CY.at[my_zl, y], crs)
    start_here(is_owner, yo.at[:, div(my_m, 2)], Y.at[:, pl.ds(gy * 64, 64)], yrs)
    start_here(is_owner, CXL, CX.at[:, lanes128], drs)

    def forward_x():
        @pl.when(is_owner)
        def _():
            wait_for(X.at[:, :, y], xrs)
            wait_for(CY.at[:, y], crs)

        x_along(start)

    @pl.when(is_flow)
    def _():
        U[...] = jnp.zeros_like(U)
        for c in range(3):
            for g in range(16):
                U[c, 2:18, 256 + 128 * g:384 + 128 * g] = f[c, :, 128 * g:128 * g + 128]
        for c in range(3):
            for j in (0, 1, 18, 19):
                V[c, :, 128 * j:128 * j + 128] = jnp.zeros((32, 128), F32)

    pl.semaphore_wait(known_x, 3)
    for d in (1, 2, 3):
        signal(known_y, device_at(x, rem(y + d, 4), z, core))

    rows8 = pl.ds(gx * 8, 8)

    def send_planes(src, t, target, recv, ready):
        first_k = rem(div(z, 2) + 1, 3)
        for i in range(3):
            k = rem(first_k + i, 3)
            if src is not None:
                relay_planes(src, t, k)
            if i == 0:
                ready()
            layers = []
            for parity in range(2):
                m = 2 * k + parity
                oz = m + (m >= 4).astype(jnp.int32)
                layers.append((m * 16, 2 * div(oz, 4) + 1, rem(oz, 4) * 4, m))
            for dx, dy in far_first():
                tx, ty = rem(x + dx, 4), rem(y + dy, 4)
                q = 4 * tx + ty
                for base, osec, ogx, m in layers:
                    copy = remote(PB.at[t, base + q], target, pss.at[t], recv, (osec, ogx + ty, tx))
                    if dx or dy:
                        copy.start()
                        continue
                    mine = is_owner & (m == my_m)

                    @pl.when(jnp.logical_not(mine))
                    def _():
                        copy.start()

                    @pl.when(mine)
                    def _():
                        pltpu.make_async_copy(PB.at[t, base + q], target, recv).start()

    def everyone():
        pl.semaphore_wait(known_y, 3)

    def drain_pieces(t):
        @pl.when(is_owner)
        def _():
            wait_for(PB.at[t, pl.ds(0, 95)], pss.at[t])

        @pl.when(jnp.logical_not(is_owner))
        def _():
            wait_for(PB.at[t], pss.at[t])

    lane = lax.broadcasted_iota(jnp.int32, (24, 128), 1)
    row = lax.broadcasted_iota(jnp.int32, (24, 128), 0)

    def mixed(lamb, k):
        at = jnp.minimum(sec, 2)
        total = coup[at, k, 0] * lamb[0] + coup[at, k, 1] * lamb[1] + coup[at, k, 2] * lamb[2]
        return time_step * total

    @pl.when(is_flow)
    def _():
        for n, (dx, dy) in enumerate(DIRS):
            rows = {-1: 0, 0: 2, 1: 18}[dx]
            lanes = {-1: 128, 0: 256, 1: 2304}[dy]

            @pl.when(inside(dx, dy))
            def _():
                if dy == 0:
                    side = 0 if dx < 0 else 1
                    wait_for(hxr.at[side], hrs.at[n])
                    for c in range(3):
                        for part in range(4):
                            U[c, rows:rows + 2, lanes + 512 * part:lanes + 512 * part + 512] = hxr[side, c, 2 * part:2 * part + 2, :]
                elif dx == 0:
                    side = 0 if dy < 0 else 1
                    wait_for(hyr.at[side], hrs.at[n])
                    for c in range(3):
                        U[c, 2:18, lanes:lanes + 128] = hyr[side, c]
                else:
                    wait_for(cr.at[n], hrs.at[n])
                    for c in range(3):
                        U[c, rows:rows + 2, lanes:lanes + 128] = cr[n, 2 * c:2 * c + 2, :]

    @pl.when(sec == 3)
    def _():
        forward_x()
        send_planes(None, 0, A.at[my_zl, y, :, lanes128], ars, everyone)

    @pl.when(is_flow)
    def _():
        valid = ((row >= 2) | (gx > 0)) & ((row < 18) | (gx < 15))

        def keep(j, updated):
            at = pl.ds(pl.multiple_of(j * 128, 128), 128)
            for c in range(3):
                rolled = roll(updated[c], -2, 0)
                V[c, 8:24, at] = rolled[0:16]
                V[c, 0:8, at] = rolled[16:24]
                V[c, 24:32, at] = rolled[16:24]

        def edge(j, there):
            updated, _ = flow_block(U, j, lane, None)
            keep(j, [jnp.where(valid & there, value, 0.0) for value in updated])

        def first(j, carry):
            updated, lamb = flow_block(U, j, lane, None)
            keep(j, [jnp.where(valid, value, 0.0) for value in updated])
            for c in range(3):
                M[c, :, pl.ds(pl.multiple_of((j - 2) * 128, 128), 128)] = roll(mixed(lamb, c), -2, 0)[0:16]
            return carry

        lax.fori_loop(2, 18, first, 0, unroll=2)
        forward_x()
        send_planes(M, 0, L.at[0, sec, rows8, lanes128], lrs.at[0, sec], everyone)

        edge(1, gy > 0)
        edge(18, gy < 3)

        def second(j, carry):
            updated, lamb = flow_block(V, j, lane[0:16], (8, 16))
            for c in range(3):
                at = pl.ds(pl.multiple_of((j - 2) * 128, 128), 128)
                out[c, :, at] = updated[c]
                M[c, :, at] = mixed(lamb, c)
            return carry

        lax.fori_loop(2, 18, second, 0, unroll=2)
        send_planes(M, 1, L.at[1, sec, rows8, lanes128], lrs.at[1, sec], lambda: None)

    @pl.when(is_owner)
    def _():
        i = lax.broadcasted_iota(jnp.int32, (256, 256), 0)
        j = lax.broadcasted_iota(jnp.int32, (256, 256), 1)
        for s in range(3):
            d = i - j - off[0, s]
            shift = jnp.where((d == 0) | (d == 1), 0.5, 0.0).astype(BF16)
            SX[:, 256 * s:256 * s + 256] = shift
            SX[:, 768 + 256 * s:1024 + 256 * s] = shift
            d = j - i - off[1, s]
            shift = jnp.where((d == 0) | (d == 1), 0.5, 0.0).astype(BF16)
            SY[s, 0:256] = shift
            SY[s, 256:512] = shift
        wait_for(X.at[:, :, pl.ds(0, 3)], xrs2)
        wait_for(CY.at[:, pl.ds(0, 3)], crs2)
        wait_for(Y, yrs)
        wait_for(CX, drs)
        for c in range(NCLASS):
            high, low = split(X[c].reshape(256, 256))
            XHH[:, 256 * c:256 * c + 256] = high
            XHH[:, 1024 + 256 * c:1280 + 256 * c] = high
            XL[:, 256 * c:256 * c + 256] = low
            high, low = split(Y[c].T)
            YHH[256 * c:256 * c + 256, :] = high
            YHH[1024 + 256 * c:1280 + 256 * c, :] = high
            YL[256 * c:256 * c + 256, :] = low

        def unpacked(ref):
            halves = []
            for h in range(2):
                a, b = pair_swap(ref[:, 256 * h:256 * h + 128], ref[:, 256 * h + 128:256 * h + 256])
                rows = jnp.stack([a.reshape(16, 8, 128), b.reshape(16, 8, 128)], axis=1)
                halves.append(rows.reshape(256, 128))
            return jnp.concatenate(halves, axis=1)

        column_class = jnp.concatenate(
            [pair_swap(CX[:, 256 * h:256 * h + 128], CX[:, 256 * h + 128:256 * h + 256])[0][0:1] for h in range(2)], axis=1
        )
        row_class = CY[...].reshape(256, 128)[:, 0:1]

        def add_source(t):
            for s in (2, 0, 1):
                wait_for(L.at[t, s], lrs.at[t, s])
            for s in range(3):
                high, low = split(unpacked(L.at[t, s]))
                high, low = split(dot(jnp.concatenate([high, low], axis=1), SY[s]))
                TT[256 * s:256 * s + 256, :] = high
                TT[768 + 256 * s:1024 + 256 * s, :] = low
            return D[...] + dot(SX[...], TT[...])

        def stack_columns(value):
            high, low = split(value)
            for c in range(NCLASS):
                keep = column_class == c
                AA[256 * c:256 * c + 256, :] = jnp.where(keep, high, jnp.zeros_like(high))
                AA[1024 + 256 * c:1280 + 256 * c, :] = jnp.where(keep, low, jnp.zeros_like(low))

        def sweeps(r, n):
            rows = slice(r, r + n)
            swept = dot(XHH[rows, :], AA[...]) + dot(XL[rows, :], AA[0:1024, :])
            high, low = split(swept)
            for c in range(NCLASS):
                keep = row_class[rows] == c
                BB[rows, 256 * c:256 * c + 256] = jnp.where(keep, high, jnp.zeros_like(high))
                BB[rows, 1024 + 256 * c:1280 + 256 * c] = jnp.where(keep, low, jnp.zeros_like(low))
            return dot(BB[rows, :], YHH[...]) + dot(BB[rows, 0:1024], YL[...])

        wait_for(A, ars)
        D[...] = unpacked(A.reshape(128, 512))
        stack_columns(add_source(0))
        D[...] = sweeps(0, 256)
        stack_columns(add_source(1))
        for part in range(PARTS):
            n = 256 // PARTS
            result = sweeps(part * n, n)
            for h in range(2):
                rows = result[:, 128 * h:128 * h + 128].reshape(n // 16, 2, 8, 128)
                a, b = pair_swap(rows[:, 0].reshape(n // 2, 128), rows[:, 1].reshape(n // 2, 128))
                R[part * n // 2:(part + 1) * n // 2, 256 * h:256 * h + 128] = a
                R[part * n // 2:(part + 1) * n // 2, 256 * h + 128:256 * h + 256] = b
            for dx, dy in far_first():
                tx, ty = rem(x + dx, 4), rem(y + dy, 4)
                for zl in range(part * 4 // PARTS, (part + 1) * 4 // PARTS):
                    rows = pl.ds(pl.multiple_of((4 * zl + ty) * 8, 8), 8)
                    src = R.at[rows, pl.ds(pl.multiple_of(tx * 128, 128), 128)]
                    copy = remote(src, Q.at[my_o], rss, rrs.at[div(my_m, 2)], (3, 4 * zl + ty, tx))
                    if dx or dy:
                        copy.start()
                        continue
                    mine = (sec == 3) & (zl == my_zl)

                    @pl.when(jnp.logical_not(mine))
                    def _():
                        copy.start()

                    @pl.when(mine)
                    def _():
                        pltpu.make_async_copy(src, Q.at[my_o], rrs.at[div(my_m, 2)]).start()

    @pl.when(sec == 3)
    def _():
        def body(k, carry):
            blocks = []
            wait_for(Q.at[pl.ds(0, 32)], rrs.at[k])
            for q in range(16):
                a, b = pair_swap(Q[32 * k + q], Q[32 * k + 16 + q])
                blocks.append(jnp.concatenate([a, b], axis=0))
            blocks = from_planes(blocks)
            for g in range(16):
                out[k, :, 128 * g:128 * g + 128] = blocks[g]
            return carry

        lax.fori_loop(0, 3, body, 0)

    @pl.when(sec == 3)
    def _():
        drain_pieces(0)

    @pl.when(is_owner & (sec == 3))
    def _():
        wait_for(Q.at[pl.ds(0, 63)], rss)

    @pl.when(is_owner & (sec != 3))
    def _():
        wait_for(Q.at[pl.ds(0, 64)], rss)

    x_column(drain)
    x_along(drain)
    y_along(drain)

    @pl.when(is_flow)
    def _():
        for n, (dx, dy) in enumerate(DIRS):
            @pl.when(inside(dx, dy))
            def _():
                halo_copy(n).wait_send()
        for t in range(2):
            drain_pieces(t)


def local(fields, x_ops, y_ops, x_line_class, y_line_class, box_offset, coupling):
    vmem, smem, any_space = (pl.BlockSpec(memory_space=m) for m in (pltpu.VMEM, pltpu.SMEM, pl.ANY))
    V, D = pltpu.VMEM, pltpu.SemaphoreType.DMA
    out = pl.pallas_call(
        kernel,
        out_shape=jax.ShapeDtypeStruct((3, 16, 2048), F32),
        in_specs=[smem, smem, any_space, any_space, any_space, vmem, vmem],
        out_specs=vmem,
        scratch_shapes=[
            V((3, 16, 2048), F32), V((3, 24, 2560), F32), V((3, 32, 2560), F32), V((3, 16, 2048), F32),
            V((2, 3, 8, 512), F32), V((2, 3, 8, 512), F32), V((2, 3, 16, 128), F32),
            V((8, 8, 128), F32), V((8, 8, 128), F32),
            V((2, 96, 8, 128), F32), V((4, 4, 8, 512), F32), V((2, 3, 128, 512), F32),
            V((4, 4, 4, 16, 256), F32), V((4, 256, 256), F32), V((4, 4, 16, 128), F32), V((8, 512), F32),
            V((16, 128), F32), V((8, 128), F32),
            V((128, 512), F32), V((256, 256), F32), V((96, 8, 128), F32),
            V((256, 2048), BF16), V((256, 1024), BF16), V((2048, 256), BF16), V((1024, 256), BF16),
            V((256, 1536), BF16), V((3, 512, 256), BF16), V((1536, 256), BF16),
            V((2048, 256), BF16), V((256, 2048), BF16),
            D, D((8,)), D((8,)), D((2,)), D, D((2, 3)),
            D((7,)), D((3,)), D((7,)), D((3,)), D, D, D, D, D, D, D, D((3,)),
            pltpu.SemaphoreType.REGULAR, pltpu.SemaphoreType.REGULAR,
        ],
        compiler_params=pltpu.CompilerParams(
            collective_id=0, has_side_effects=True, vmem_limit_bytes=60 << 20
        ),
    )(coupling, box_offset.T, fields[0], x_ops, y_ops, x_line_class[None], y_line_class[None])
    return out[None]


def solution(mesh):
    placed = (
        P("sec", None, "gx", "gy"),
        P(None, None, "gx", None),
        P(None, None, "gy", None),
        P("gy"),
        P("gx"),
        P(),
        P(),
    )
    return jax.shard_map(
        local, mesh=mesh, in_specs=placed, out_specs=P("sec", None, "gx", "gy"), check_vma=False
    )
```
